512 devices in a mesh: pipe: 32 (over y, x, core), dp: 16 (over z).
Axes of the slice: x: 4, y: 4, z: 16, core: 2. Of those that a mesh axis runs over, the one named last changes fastest.
Arguments:
- x_saved: bfloat16 [32, 4096, 1024], P('pipe', 'dp'), may hold values from -6 to 6
- up_weights: bfloat16 [32, 1024, 2048], P('pipe', 'dp'), may hold values from -0.1875 to 0.1875
- down_weights: bfloat16 [32, 2048, 1024], P('pipe', 'dp'), may hold values from -0.125 to 0.125
- norm_gain: float32 [32, 1024], P('pipe'), may hold values from 0.1 to 1.9
- layer_scale: float32 [32, 1024], P('pipe'), may hold values from 0.1 to 1
- cotangent: bfloat16 [4096, 1024], P('dp'), may hold values from -0.119628906 to 0.119628906
- lengths: int32 [16, 2], P('dp'), may hold values from 1 to 128, 160 in all within a row
Outputs:
- weight_grad: bfloat16 [32, 2048, 1024], P('pipe', 'dp')
- gain_grad: float32 [32, 1024], P('pipe')
- scale_grad: float32 [32, 1024], P('pipe')
The draws below stay inside these ranges and needn't reach their ends.
Inputs may be any that keep to these rules, and one draw needn't show every extreme that they name: `lengths`: each row sums to 128 * M * 5 // 8.
All inputs are finite; a program needn't handle non-finite values.
Results may differ from the reference program's by a relative error of at most 0.04.
Values may be sent and summed in bfloat16 or wider, within the bound.
A program may use at most 64 MiB of HBM per device.

```python
import math
import jax
import jax.numpy as jnp
import numpy as np
from jax import lax

D = 1024
FF = 2048
M = 2
SLOT = 128
LAYERS = 32
UTTS = 16
TOKENS = 4096
N_DP = 16


def spiked(array, stream_key, source, target, blocks, factor):
    owner, partner = [(jnp.arange(array.shape[dim]) // (array.shape[dim] // blocks)).reshape([-1 if axis == dim else 1 for axis in range(array.ndim)]) for dim in (source, target)]
    chosen = jax.random.permutation(stream_key, blocks)[partner]
    strong = (owner == chosen) | (owner == (partner + blocks // 2) % blocks)
    return jnp.where(strong, factor * array, array)


def shard_levels(rng, extent, split, least, top_value):
    gain, own = 1.0, jax.random.fold_in(rng, 6)
    for dim, blocks in split:
        draws = jnp.exp(jax.random.uniform(jax.random.fold_in(own, dim), (blocks,), jnp.float32, least / len(split), top_value / len(split)))
        gain = gain * jnp.repeat(draws, extent[dim] // blocks).reshape([-1 if axis == dim else 1 for axis in range(len(extent))])
    return gain


def profile(number_of, total, reach, lean):
    loads = [(1 << 20) // math.isqrt(grade ** lean) + 1 for grade in range(2, number_of + 1)]
    spare, holding = total - reach - (number_of - 1), [1] * (number_of - 1)
    while spare > 0:
        free = [i for i in range(number_of - 1) if holding[i] < reach]
        mass, budget = sum([loads[i] for i in free]), spare
        for i in free:
            extra = min(reach - holding[i], max(1, budget * loads[i] // mass), spare)
            holding[i] = holding[i] + extra
            spare = spare - extra
    return np.array([reach] + holding)


def ragged(stream_key, count, total, reach, lean):
    if count == 2:
        one = jax.random.randint(stream_key, (), max(1, total - reach), min(reach, total - 1) + 1)
        return jnp.stack([one, total - one])
    sizes = jnp.asarray(profile(count, total, reach, lean), jnp.int32)
    pairs = (count - 1) // 2
    source_of, sink = sizes[1:1 + 2 * pairs:2], sizes[2:2 + 2 * pairs:2]
    margin = jnp.minimum(source_of - 1, reach - sink)
    shifted = jax.random.randint(jax.random.fold_in(stream_key, 1), (pairs,), 0, 1 << 20) % (margin + 1)
    sizes = sizes.at[1:1 + 2 * pairs:2].set(source_of - shifted).at[2:2 + 2 * pairs:2].set(sink + shifted)
    return sizes[jax.random.permutation(jax.random.fold_in(stream_key, 2), count)]


def scatter_about(rng, shape, width, most, shards=(), held_as=jnp.bfloat16):
    entries = jax.random.normal(rng, shape, jnp.float32) * width
    if len(shards) > 0:
        entries = shard_levels(rng, shape, shards, -0.22, 0.18) * entries
    return jnp.clip(entries, min=-most, max=most).astype(held_as)


def noise_with(rng, shape, spread, limit, shards, heavy, held_as=jnp.bfloat16):
    drawn = spread * jax.random.normal(rng, shape, jnp.float32)
    if shards:
        drawn = drawn * shard_levels(rng, shape, shards, -0.22, 0.18)
    return jnp.clip(spiked(drawn, jax.random.fold_in(rng, 3), *heavy), -limit, limit).astype(held_as)


def setup_inputs(seed: int = 0) -> dict:
    key_list = jax.random.split(jax.random.key(seed), 8)
    x_saved = noise_with(key_list[0], (LAYERS, TOKENS, D), 1.0, 6.0, ((0, 32), (1, 16)), (1, 2, 16, 2.0))
    up_weights = scatter_about(key_list[1], (LAYERS, D, FF), D ** -0.5, 0.1875, ((0, 32), (1, 16)))
    down_weights = scatter_about(key_list[2], (LAYERS, FF, D), FF ** -0.5, 0.125, ((0, 32), (1, 16)))
    norm_gain = jnp.clip(1.0 + 0.18 * jax.random.normal(key_list[3], (LAYERS, D), jnp.float32), 0.1, 1.9)
    layer_scale = jnp.clip(jnp.exp(math.log(1.0) - 2.3025851 * jax.random.uniform(key_list[4], (LAYERS, D), jnp.float32) ** shard_levels(key_list[4], (LAYERS, D), ((0, 32),), -0.2, 0.2)), 0.1, 1.0)
    cotangent = scatter_about(key_list[5], (TOKENS, D), 0.02, 0.119628906, ((0, 16),))
    lengths = jax.vmap(lambda own: ragged(own, M, SLOT * M * 5 // 8, SLOT, 0))(jax.random.split(key_list[6], UTTS)).reshape((UTTS, M)).astype(jnp.int32)
    return {"x_saved": x_saved, "up_weights": up_weights, "down_weights": down_weights, "norm_gain": norm_gain, "layer_scale": layer_scale, "cotangent": cotangent, "lengths": lengths}


epsilon = 1e-06

def gelu_tanh(values):
    return jax.nn.gelu(values, approximate=True)

def layer_back(x_rows, incoming, up_weight, down_weight, gain_vec, scale_vec):
    x_float = x_rows.astype(jnp.float32)
    inverse = lax.rsqrt(lax.optimization_barrier(jnp.mean(x_float * x_float, axis=-1, keepdims=True)) + epsilon)
    unit = x_float * inverse
    normed = (unit * gain_vec).astype(jnp.bfloat16)
    hidden = jnp.dot(normed, up_weight, preferred_element_type=jnp.float32)
    active, gelu_back = jax.vjp(gelu_tanh, hidden)
    act = active.astype(jnp.bfloat16)
    branch = jnp.dot(act, down_weight, preferred_element_type=jnp.float32)
    upper = incoming.astype(jnp.float32)
    scale_part = lax.optimization_barrier(jnp.sum(upper * branch, axis=0))
    branch_grad = (upper * scale_vec).astype(jnp.bfloat16)
    act_grad = jnp.dot(branch_grad, down_weight.T, preferred_element_type=jnp.float32)
    hidden_grad = gelu_back(act_grad)[0].astype(jnp.bfloat16)
    normed_grad = jnp.dot(hidden_grad, up_weight.T, preferred_element_type=jnp.float32)
    gain_part = lax.optimization_barrier(jnp.sum(normed_grad * unit, axis=0))
    unit_grad = normed_grad * gain_vec
    back_rows = (upper + inverse * (unit_grad - unit * lax.optimization_barrier(jnp.mean(unit_grad * unit, axis=-1, keepdims=True)))).astype(jnp.bfloat16)
    return (act, branch_grad, back_rows, gain_part, scale_part)

def reference(x_saved, up_weights, down_weights, norm_gain, layer_scale, cotangent, lengths):
    token_ids = jnp.arange(TOKENS, dtype=jnp.int32)
    position = token_ids % SLOT
    owner = token_ids // SLOT
    valid = position < lengths.reshape(-1)[owner]
    start_grad = jnp.where(valid[:, None], cotangent, jnp.zeros_like(cotangent))

    def one_layer(incoming, layer):
        x_rows, up_weight, down_weight, gain_vec, scale_vec = layer
        act, branch_grad, back_rows, gain_part, scale_part = layer_back(x_rows, incoming, up_weight, down_weight, gain_vec, scale_vec)
        act_split = act.reshape(N_DP, -1, FF)
        grad_split = branch_grad.reshape(N_DP, -1, D)

        def partial_of(pair):
            return lax.dot_general(pair[0], pair[1], (((0,), (0,)), ((), ())), preferred_element_type=jnp.float32).astype(jnp.bfloat16)
        partials = lax.map(partial_of, (act_split, grad_split))
        partials = lax.optimization_barrier(partials)
        weight_part = lax.optimization_barrier(jnp.sum(partials.astype(jnp.float32), axis=0)).astype(jnp.bfloat16)
        return (back_rows, (weight_part, gain_part, scale_part))
    unused, outputs = lax.scan(one_layer, start_grad, (x_saved, up_weights, down_weights, norm_gain, layer_scale), reverse=True)
    return (outputs[0], outputs[1], outputs[2])
```

```python
import functools

import jax
import jax.numpy as jnp
from jax import lax
from jax.experimental import pallas as pl
from jax.experimental.pallas import tpu as pltpu
from jax.sharding import PartitionSpec as P

EPSILON = 1e-06
ROOT = 0.7978845608028654
CUBIC = 0.044715
PIECES = 5
CHUNKS = 4
F_TILE = 512
LAG = 2
MESH = pl.DeviceIdType.MESH
NT = (((1,), (1,)), ((), ()))
F32 = jnp.float32
BF16 = jnp.bfloat16


def kernel(
    stages,
    ring,
    len_ref,
    up_ref,
    down_ref,
    x_ref,
    cot_ref,
    gain_ref,
    scale_ref,
    out_ref,
    gain_out,
    scale_out,
    up_w,
    down_w,
    hidden,
    slope,
    act,
    act_t,
    unit,
    inverse,
    normed,
    branch,
    start,
    g_in,
    back,
    bg,
    hg,
    gain_acc,
    stats,
    rs_send_a,
    rs_recv_a,
    rs_send_b,
    rs_recv_b,
    up_sems,
    down_sems,
    chain_sems,
    rs_sems,
    stat_sems,
):
    s = lax.axis_index("pipe")
    z = lax.axis_index("dp")
    last = stages - 1
    right = lax.rem(z + 1, ring)
    left = lax.rem(z + ring - 1, ring)
    above = lax.rem(s + 1, stages)
    below = lax.rem(s + stages - 1, stages)
    width, ff = up_w.shape
    up_rows = up_ref.shape[1]
    down_rows = down_ref.shape[1]
    tokens = normed.shape[0]
    slot = x_ref.shape[1] // 2
    hops_a = ring // 2
    hops_b = ring - 1 - hops_a
    piece_rows = tokens // PIECES
    chunk = width // CHUNKS

    barrier = pltpu.get_barrier_semaphore()
    for place in ({"dp": right}, {"dp": left}, {"pipe": above}, {"pipe": below}):
        pl.semaphore_signal(barrier, inc=1, device_id=place, device_id_type=MESH)
    pl.semaphore_wait(barrier, 4)

    def shard(buffer, rows, owner):
        return buffer.at[pl.ds(pl.multiple_of(owner * rows, rows), rows)]

    def gather_copy(buffer, rows, sems, way, step, first=None):
        owner = lax.rem(z - step + ring, ring) if way == 0 else lax.rem(z + step, ring)
        block = shard(buffer, rows, owner)
        return pltpu.make_async_remote_copy(
            src_ref=block if first is None else first,
            dst_ref=block,
            send_sem=sems.at[0, way, step],
            recv_sem=sems.at[1, way, step],
            device_id={"dp": right if way == 0 else left},
            device_id_type=MESH,
        )

    def gather_arrival(buffer, rows, sems, way, step):
        owner = lax.rem(z - 1 - step + ring, ring) if way == 0 else lax.rem(z + 1 + step, ring)
        block = shard(buffer, rows, owner)
        return pltpu.make_async_remote_copy(
            src_ref=block,
            dst_ref=block,
            send_sem=sems.at[0, way, step],
            recv_sem=sems.at[1, way, step],
            device_id={"dp": right if way == 0 else left},
            device_id_type=MESH,
        )

    weights = (
        (up_w, up_rows, up_sems, up_ref.at[0]),
        (down_w, down_rows, down_sems, down_ref.at[0]),
    )

    def gather_step(which, step):
        buffer, rows, sems, own = weights[which]
        for way, hops in ((0, hops_a), (1, hops_b)):
            if step > 0 and step <= hops:
                gather_arrival(buffer, rows, sems, way, step - 1).wait_recv()
            if step < hops:
                gather_copy(
                    buffer, rows, sems, way, step, own if step == 0 else None
                ).start()

    gather_step(0, 0)
    for buffer, rows, sems, own in weights:
        shard(buffer, rows, z)[...] = own[...]

    first_len = len_ref[0, 0]
    row = lax.broadcasted_iota(jnp.int32, (tokens, x_ref.shape[1]), 0)
    col = lax.broadcasted_iota(jnp.int32, (tokens, x_ref.shape[1]), 1)
    source = jnp.where(row < first_len, row, row + (slot - first_len))
    pick = (col == source).astype(F32).astype(BF16)
    x_rows = jnp.dot(pick, x_ref[0], preferred_element_type=F32)
    scaled = lax.rsqrt(jnp.mean(x_rows * x_rows, axis=-1, keepdims=True) + EPSILON)
    inverse[...] = jnp.broadcast_to(scaled, inverse.shape)
    unit_rows = x_rows * scaled
    unit[...] = unit_rows
    normed[...] = (unit_rows * gain_ref[...]).astype(BF16)
    start[...] = jnp.dot(pick, cot_ref[...], preferred_element_type=F32).astype(BF16)
    gain_acc[...] = jnp.zeros_like(gain_acc)

    def hidden_tile(tile):
        cols = pl.ds(pl.multiple_of(tile * F_TILE, F_TILE), F_TILE)
        h = jnp.dot(normed[...], up_w[:, cols], preferred_element_type=F32)
        square = h * h
        th = jnp.tanh(ROOT * (h + CUBIC * (square * h)))
        half = 0.5 * (1.0 + th)
        a = h * half
        hidden[:, cols] = h
        slope[:, cols] = half + 0.5 * h * (1.0 - th * th) * (
            ROOT * (1.0 + (3.0 * CUBIC) * square)
        )
        act[:, cols] = a.astype(BF16)
        act_t[cols, :] = a.T.astype(BF16)

    tiles = ff // F_TILE
    for step in range(1, hops_a + LAG + 1):
        if step <= hops_a:
            gather_step(0, step)
        if step >= LAG:
            gather_step(1, step - LAG)
        if step >= hops_a and step < hops_a + LAG:
            part = step - hops_a
            lax.fori_loop(
                part * tiles // LAG,
                (part + 1) * tiles // LAG,
                lambda tile, c: (hidden_tile(tile), c)[1],
                0,
            )

    @pl.when(s == last)
    def _():
        for c in range(CHUNKS):
            g_in[c] = start[:, c * chunk : (c + 1) * chunk]

    def branch_tile(tile, carry):
        cols = pl.ds(pl.multiple_of(tile * F_TILE, F_TILE), F_TILE)
        branch[:, cols] = jnp.dot(act[...], down_w[:, cols], preferred_element_type=F32)
        return carry

    @pl.when(s < last)
    def _():
        lax.fori_loop(0, width // F_TILE, branch_tile, 0)

    def chain_copy(p, c):
        rows = pl.ds(pl.multiple_of(p * piece_rows, piece_rows), piece_rows)
        return pltpu.make_async_remote_copy(
            src_ref=back.at[c, rows],
            dst_ref=g_in.at[c, rows],
            send_sem=chain_sems.at[0, p, c],
            recv_sem=chain_sems.at[1, p, c],
            device_id={"pipe": below},
            device_id_type=MESH,
        )

    def piece(p, carry):
        rows = pl.ds(pl.multiple_of(p * piece_rows, piece_rows), piece_rows)
        for c in range(CHUNKS):

            @pl.when(s < last)
            def _():
                chain_copy(p, c).wait_recv()

            cols = slice(c * chunk, (c + 1) * chunk)
            bg[rows, cols] = (g_in[c, rows].astype(F32) * scale_ref[:, cols]).astype(BF16)
        grad = bg[rows, :]
        total = jnp.zeros((piece_rows, 1), F32)
        for f in range(tiles):
            cols = slice(f * F_TILE, (f + 1) * F_TILE)
            act_grad = lax.dot_general(grad, down_w[cols, :], NT, preferred_element_type=F32)
            rounded = (act_grad * slope[rows, cols]).astype(BF16)
            hg[rows, cols] = rounded
            total += jnp.sum(rounded.astype(F32) * hidden[rows, cols], axis=-1, keepdims=True)
        mean = total * (1.0 / width)
        inv = inverse[rows, 0:1]
        hidden_grad = hg[rows, :]
        for c in range(CHUNKS):
            cols = slice(c * chunk, (c + 1) * chunk)
            normed_grad = lax.dot_general(
                hidden_grad, up_w[cols, :], NT, preferred_element_type=F32
            )
            unit_part = unit[rows, cols]
            back[c, rows] = (
                g_in[c, rows].astype(F32)
                + inv * (normed_grad * gain_ref[:, cols] - unit_part * mean)
            ).astype(BF16)

            @pl.when(s > 0)
            def _():
                chain_copy(p, c).start()

            gain_acc[:, cols] += jnp.sum(normed_grad * unit_part, axis=0, keepdims=True)
        return carry

    lax.fori_loop(0, PIECES, piece, 0)

    @pl.when(s == last)
    def _():
        lax.fori_loop(0, width // F_TILE, branch_tile, 0)

    stats[z, 0:1, :] = gain_acc[...]
    for c in range(CHUNKS):
        cols = slice(c * chunk, (c + 1) * chunk)
        stats[z, 1:2, cols] = jnp.sum(
            g_in[c].astype(F32) * branch[:, cols], axis=0, keepdims=True
        )

    def own_part(dest):
        rows = pl.ds(pl.multiple_of(dest * down_rows, down_rows), down_rows)
        return jnp.dot(act_t[rows, :], bg[...], preferred_element_type=F32)

    ways = (
        (0, hops_a, rs_send_a, rs_recv_a, right),
        (1, hops_b, rs_send_b, rs_recv_b, left),
    )

    def rs_copy(way, j):
        number, hops, sent, received, target = ways[way]
        return pltpu.make_async_remote_copy(
            src_ref=sent.at[j],
            dst_ref=received.at[j],
            send_sem=rs_sems.at[0, way, j],
            recv_sem=rs_sems.at[1, way, j],
            device_id={"dp": target},
            device_id_type=MESH,
        )

    def stat_copy(way, j, arrival=False):
        ahead = j + 1 if arrival else j
        owner = lax.rem(z - ahead + ring, ring) if way == 0 else lax.rem(z + ahead, ring)
        return pltpu.make_async_remote_copy(
            src_ref=stats.at[owner],
            dst_ref=stats.at[owner],
            send_sem=stat_sems.at[0, way, j],
            recv_sem=stat_sems.at[1, way, j],
            device_id={"dp": right if way == 0 else left},
            device_id_type=MESH,
        )

    def rs_step(j, carry):
        for way, hops, sent, received, target in ways:

            @pl.when(j < hops)
            def _():
                ahead = hops - j
                dest = lax.rem(z + ahead, ring) if way == 0 else lax.rem(z - ahead + ring, ring)
                value = own_part(dest)

                @pl.when(j == 0)
                def _():
                    sent[j] = value.astype(BF16)

                @pl.when(j > 0)
                def _():
                    rs_copy(way, j - 1).wait_recv()
                    sent[j] = (value + received[j - 1].astype(F32)).astype(BF16)

                rs_copy(way, j).start()

                @pl.when(j > 0)
                def _():
                    stat_copy(way, j - 1, True).wait_recv()

                stat_copy(way, j).start()

        return carry

    lax.fori_loop(0, hops_a, rs_step, 0)
    value = own_part(z)
    for way, hops, sent, received, target in ways:
        rs_copy(way, hops - 1).wait_recv()
        value = value + received[hops - 1].astype(F32)
        stat_copy(way, hops - 1, True).wait_recv()
    out_ref[0] = value.astype(BF16)
    summed = stats[0]
    for i in range(1, ring):
        summed = summed + stats[i]
    gain_out[...] = summed[0:1]
    scale_out[...] = summed[1:2]

    for way, hops in ((0, hops_a), (1, hops_b)):
        for step in range(hops):
            for buffer, rows, sems, own in weights:
                gather_copy(
                    buffer, rows, sems, way, step, own if step == 0 else None
                ).wait_send()
            rs_copy(way, step).wait_send()
            stat_copy(way, step).wait_send()

    @pl.when(s > 0)
    def _():
        for p in range(PIECES):
            for c in range(CHUNKS):
                chain_copy(p, c).wait_send()


def shards(stages, ring, x_saved, up_weights, down_weights, norm_gain, layer_scale, cotangent, lengths):
    unused, rows, width = x_saved.shape
    ff = up_weights.shape[2]
    down_rows = down_weights.shape[1]
    tokens = rows * 5 // 8
    hops_a = ring // 2
    hops_b = ring - 1 - hops_a
    vmem = pl.BlockSpec(memory_space=pltpu.VMEM)
    smem = pl.BlockSpec(memory_space=pltpu.SMEM)
    return pl.pallas_call(
        functools.partial(kernel, stages, ring),
        out_shape=(
            jax.ShapeDtypeStruct((1, down_rows, width), BF16),
            jax.ShapeDtypeStruct((1, width), F32),
            jax.ShapeDtypeStruct((1, width), F32),
        ),
        in_specs=[smem] + [vmem] * 6,
        out_specs=(vmem, vmem, vmem),
        scratch_shapes=[
            pltpu.VMEM((width, ff), BF16),
            pltpu.VMEM((ff, width), BF16),
            pltpu.VMEM((tokens, ff), F32),
            pltpu.VMEM((tokens, ff), F32),
            pltpu.VMEM((tokens, ff), BF16),
            pltpu.VMEM((ff, tokens), BF16),
            pltpu.VMEM((tokens, width), F32),
            pltpu.VMEM((tokens, 128), F32),
            pltpu.VMEM((tokens, width), BF16),
            pltpu.VMEM((tokens, width), F32),
            pltpu.VMEM((tokens, width), BF16),
            pltpu.VMEM((CHUNKS, tokens, width // CHUNKS), BF16),
            pltpu.VMEM((CHUNKS, tokens, width // CHUNKS), BF16),
            pltpu.VMEM((tokens, width), BF16),
            pltpu.VMEM((tokens, ff), BF16),
            pltpu.VMEM((1, width), F32),
            pltpu.VMEM((ring, 2, width), F32),
            pltpu.VMEM((hops_a, down_rows, width), BF16),
            pltpu.VMEM((hops_a, down_rows, width), BF16),
            pltpu.VMEM((hops_b, down_rows, width), BF16),
            pltpu.VMEM((hops_b, down_rows, width), BF16),
            pltpu.SemaphoreType.DMA((2, 2, hops_a)),
            pltpu.SemaphoreType.DMA((2, 2, hops_a)),
            pltpu.SemaphoreType.DMA((2, PIECES, CHUNKS)),
            pltpu.SemaphoreType.DMA((2, 2, hops_a)),
            pltpu.SemaphoreType.DMA((2, 2, hops_a)),
        ],
        compiler_params=pltpu.CompilerParams(
            collective_id=0, has_side_effects=True, vmem_limit_bytes=60 * 1024 * 1024
        ),
        name="layer_chain",
    )(lengths, up_weights, down_weights, x_saved, cotangent, norm_gain, layer_scale)


def solution(mesh):
    return jax.shard_map(
        functools.partial(shards, mesh.shape["pipe"], mesh.shape["dp"]),
        mesh=mesh,
        in_specs=(
            P("pipe", "dp", None),
            P("pipe", "dp", None),
            P("pipe", "dp", None),
            P("pipe", None),
            P("pipe", None),
            P("dp", None),
            P("dp", None),
        ),
        out_specs=(P("pipe", "dp", None), P("pipe", None), P("pipe", None)),
        check_vma=False,
    )
```

```python
import functools

import jax
import jax.numpy as jnp
from jax import lax
from jax.experimental import pallas as pl
from jax.experimental.pallas import tpu as pltpu
from jax.sharding import PartitionSpec as P

EPSILON = 1e-06
ROOT = 0.7978845608028654
CUBIC = 0.044715
PIECES = 5
CHUNKS = 2
F_TILE = 512
LAG = 2
MESH = pl.DeviceIdType.MESH
F32 = jnp.float32
BF16 = jnp.bfloat16


def kernel(
    stages,
    ring,
    len_ref,
    up_ref,
    down_ref,
    x_ref,
    cot_ref,
    gain_ref,
    scale_ref,
    out_ref,
    gain_out,
    scale_out,
    up_w,
    down_w,
    up_t,
    down_t,
    hidden,
    slope,
    act,
    act_t,
    unit,
    inverse,
    normed,
    branch,
    start,
    g_in,
    back,
    bg,
    hg,
    gain_acc,
    stats,
    rs_send_a,
    rs_recv_a,
    rs_send_b,
    rs_recv_b,
    up_sems,
    down_sems,
    chain_sems,
    rs_sems,
    stat_sems,
):
    s = lax.axis_index("pipe")
    z = lax.axis_index("dp")
    last = stages - 1
    right = lax.rem(z + 1, ring)
    left = lax.rem(z + ring - 1, ring)
    above = lax.rem(s + 1, stages)
    below = lax.rem(s + stages - 1, stages)
    width, ff = up_w.shape
    up_rows = up_ref.shape[1]
    down_rows = down_ref.shape[1]
    tokens = normed.shape[0]
    slot = x_ref.shape[1] // 2
    hops_a = ring // 2
    hops_b = ring - 1 - hops_a
    piece_rows = tokens // PIECES
    chunk = width // CHUNKS

    barrier = pltpu.get_barrier_semaphore()
    for place in ({"dp": right}, {"dp": left}, {"pipe": above}, {"pipe": below}):
        pl.semaphore_signal(barrier, inc=1, device_id=place, device_id_type=MESH)
    pl.semaphore_wait(barrier, 4)

    def shard(buffer, rows, owner):
        return buffer.at[pl.ds(pl.multiple_of(owner * rows, rows), rows)]

    def gather_copy(buffer, rows, sems, way, step, first=None):
        owner = lax.rem(z - step + ring, ring) if way == 0 else lax.rem(z + step, ring)
        block = shard(buffer, rows, owner)
        return pltpu.make_async_remote_copy(
            src_ref=block if first is None else first,
            dst_ref=block,
            send_sem=sems.at[0, way, step],
            recv_sem=sems.at[1, way, step],
            device_id={"dp": right if way == 0 else left},
            device_id_type=MESH,
        )

    def gather_arrival(buffer, rows, sems, way, step):
        owner = lax.rem(z - 1 - step + ring, ring) if way == 0 else lax.rem(z + 1 + step, ring)
        block = shard(buffer, rows, owner)
        return pltpu.make_async_remote_copy(
            src_ref=block,
            dst_ref=block,
            send_sem=sems.at[0, way, step],
            recv_sem=sems.at[1, way, step],
            device_id={"dp": right if way == 0 else left},
            device_id_type=MESH,
        )

    weights = (
        (up_w, up_rows, up_sems, up_ref.at[0]),
        (down_w, down_rows, down_sems, down_ref.at[0]),
    )

    def gather_step(which, step):
        buffer, rows, sems, own = weights[which]
        for way, hops in ((0, hops_a), (1, hops_b)):
            if step > 0 and step <= hops:
                gather_arrival(buffer, rows, sems, way, step - 1).wait_recv()
            if step < hops:
                gather_copy(
                    buffer, rows, sems, way, step, own if step == 0 else None
                ).start()

    gather_step(0, 0)
    for buffer, rows, sems, own in weights:
        shard(buffer, rows, z)[...] = own[...]

    first_len = len_ref[0, 0]
    row = lax.broadcasted_iota(jnp.int32, (tokens, x_ref.shape[1]), 0)
    col = lax.broadcasted_iota(jnp.int32, (tokens, x_ref.shape[1]), 1)
    source = jnp.where(row < first_len, row, row + (slot - first_len))
    pick = (col == source).astype(F32).astype(BF16)
    x_rows = jnp.dot(pick, x_ref[0], preferred_element_type=F32)
    scaled = lax.rsqrt(jnp.mean(x_rows * x_rows, axis=-1, keepdims=True) + EPSILON)
    inverse[...] = jnp.broadcast_to(scaled, inverse.shape)
    unit_rows = x_rows * scaled
    unit[...] = unit_rows
    normed[...] = (unit_rows * gain_ref[...]).astype(BF16)
    start[...] = jnp.dot(pick, cot_ref[...], preferred_element_type=F32).astype(BF16)
    gain_acc[...] = jnp.zeros_like(gain_acc)

    def hidden_tile(tile):
        cols = pl.ds(pl.multiple_of(tile * F_TILE, F_TILE), F_TILE)
        h = jnp.dot(normed[...], up_w[:, cols], preferred_element_type=F32)
        square = h * h
        th = jnp.tanh(ROOT * (h + CUBIC * (square * h)))
        half = 0.5 * (1.0 + th)
        a = h * half
        hidden[:, cols] = h
        slope[:, cols] = half + 0.5 * h * (1.0 - th * th) * (
            ROOT * (1.0 + (3.0 * CUBIC) * square)
        )
        act[:, cols] = a.astype(BF16)
        act_t[cols, :] = a.T.astype(BF16)

    def turn_up(block, carry):
        rows = pl.ds(pl.multiple_of(block * 128, 128), 128)
        up_t[:, rows] = up_w[rows, :].T
        return carry

    def turn_down(owner):
        for part in range(down_rows // 128):
            rows = pl.ds(pl.multiple_of(owner * down_rows + part * 128, 128), 128)
            down_t[:, rows] = down_w[rows, :].T

    turn_down(z)
    blocks = width // 128
    tiles = ff // F_TILE
    for step in range(1, hops_a + LAG + 1):
        if step <= hops_a:
            gather_step(0, step)
        if step >= LAG:
            gather_step(1, step - LAG)
            done = step - LAG
            if done > 0 and done <= hops_a:
                turn_down(lax.rem(z - done + ring, ring))
            if done > 0 and done <= hops_b:
                turn_down(lax.rem(z + done, ring))
        if step >= hops_a and step < hops_a + LAG:
            part = step - hops_a
            lax.fori_loop(
                part * tiles // LAG,
                (part + 1) * tiles // LAG,
                lambda tile, c: (hidden_tile(tile), c)[1],
                0,
            )
            lax.fori_loop(part * blocks // LAG, (part + 1) * blocks // LAG, turn_up, 0)

    @pl.when(s == last)
    def _():
        for c in range(CHUNKS):
            g_in[0, c] = start[:, c * chunk : (c + 1) * chunk]

    def branch_tile(tile, carry):
        cols = pl.ds(pl.multiple_of(tile * F_TILE, F_TILE), F_TILE)
        branch[:, cols] = jnp.dot(act[...], down_w[:, cols], preferred_element_type=F32)
        return carry

    @pl.when(s < last)
    def _():
        lax.fori_loop(0, width // F_TILE, branch_tile, 0)

    landing = jnp.where(s == 0, 1, 0)

    def chain_copy(p, c):
        rows = pl.ds(pl.multiple_of(p * piece_rows, piece_rows), piece_rows)
        return pltpu.make_async_remote_copy(
            src_ref=back.at[c, rows],
            dst_ref=g_in.at[landing, c, rows],
            send_sem=chain_sems.at[0, p, c],
            recv_sem=chain_sems.at[1, p, c],
            device_id={"pipe": below},
            device_id_type=MESH,
        )

    def chain_arrival(p, c, slot):
        rows = pl.ds(pl.multiple_of(p * piece_rows, piece_rows), piece_rows)
        return pltpu.make_async_remote_copy(
            src_ref=back.at[c, rows],
            dst_ref=g_in.at[slot, c, rows],
            send_sem=chain_sems.at[0, p, c],
            recv_sem=chain_sems.at[1, p, c],
            device_id={"pipe": below},
            device_id_type=MESH,
        )

    def piece(p, carry):
        rows = pl.ds(pl.multiple_of(p * piece_rows, piece_rows), piece_rows)

        @pl.when(s < last)
        def _():
            for c in range(CHUNKS):
                chain_arrival(p, c, 0).wait_recv()

        for c in range(CHUNKS):
            cols = slice(c * chunk, (c + 1) * chunk)
            bg[rows, cols] = (g_in[0, c, rows].astype(F32) * scale_ref[:, cols]).astype(BF16)
        grad = bg[rows, :]
        total = jnp.zeros((piece_rows, 1), F32)
        for f in range(tiles):
            cols = slice(f * F_TILE, (f + 1) * F_TILE)
            act_grad = jnp.dot(grad, down_t[:, cols], preferred_element_type=F32)
            rounded = (act_grad * slope[rows, cols]).astype(BF16)
            hg[rows, cols] = rounded
            total += jnp.sum(rounded.astype(F32) * hidden[rows, cols], axis=-1, keepdims=True)
        mean = total * (1.0 / width)
        inv = inverse[rows, 0:1]
        hidden_grad = hg[rows, :]
        for c in range(CHUNKS):
            cols = slice(c * chunk, (c + 1) * chunk)
            normed_grad = jnp.dot(hidden_grad, up_t[:, cols], preferred_element_type=F32)
            unit_part = unit[rows, cols]
            back[c, rows] = (
                g_in[0, c, rows].astype(F32)
                + inv * (normed_grad * gain_ref[:, cols] - unit_part * mean)
            ).astype(BF16)
            chain_copy(p, c).start()
            gain_acc[:, cols] += jnp.sum(normed_grad * unit_part, axis=0, keepdims=True)
        return carry

    lax.fori_loop(0, PIECES, piece, 0)

    @pl.when(s == last)
    def _():
        lax.fori_loop(0, width // F_TILE, branch_tile, 0)

    stats[z, 0:1, :] = gain_acc[...]
    for c in range(CHUNKS):
        cols = slice(c * chunk, (c + 1) * chunk)
        stats[z, 1:2, cols] = jnp.sum(
            g_in[0, c].astype(F32) * branch[:, cols], axis=0, keepdims=True
        )

    def own_part(dest):
        rows = pl.ds(pl.multiple_of(dest * down_rows, down_rows), down_rows)
        return jnp.dot(act_t[rows, :], bg[...], preferred_element_type=F32)

    ways = (
        (0, hops_a, rs_send_a, rs_recv_a, right),
        (1, hops_b, rs_send_b, rs_recv_b, left),
    )

    def rs_copy(way, j):
        number, hops, sent, received, target = ways[way]
        return pltpu.make_async_remote_copy(
            src_ref=sent.at[j],
            dst_ref=received.at[j],
            send_sem=rs_sems.at[0, way, j],
            recv_sem=rs_sems.at[1, way, j],
            device_id={"dp": target},
            device_id_type=MESH,
        )

    def stat_copy(way, j, arrival=False):
        ahead = j + 1 if arrival else j
        owner = lax.rem(z - ahead + ring, ring) if way == 0 else lax.rem(z + ahead, ring)
        return pltpu.make_async_remote_copy(
            src_ref=stats.at[owner],
            dst_ref=stats.at[owner],
            send_sem=stat_sems.at[0, way, j],
            recv_sem=stat_sems.at[1, way, j],
            device_id={"dp": right if way == 0 else left},
            device_id_type=MESH,
        )

    def rs_step(j, carry):
        for way, hops, sent, received, target in ways:

            @pl.when(j < hops)
            def _():
                ahead = hops - j
                dest = lax.rem(z + ahead, ring) if way == 0 else lax.rem(z - ahead + ring, ring)
                value = own_part(dest)

                @pl.when(j == 0)
                def _():
                    sent[j] = value.astype(BF16)

                @pl.when(j > 0)
                def _():
                    rs_copy(way, j - 1).wait_recv()
                    sent[j] = (value + received[j - 1].astype(F32)).astype(BF16)

                rs_copy(way, j).start()

                @pl.when(j > 0)
                def _():
                    stat_copy(way, j - 1, True).wait_recv()

                stat_copy(way, j).start()

        return carry

    lax.fori_loop(0, hops_a, rs_step, 0)
    value = own_part(z)
    for way, hops, sent, received, target in ways:
        rs_copy(way, hops - 1).wait_recv()
        value = value + received[hops - 1].astype(F32)
        stat_copy(way, hops - 1, True).wait_recv()
    out_ref[0] = value.astype(BF16)
    summed = stats[0]
    for i in range(1, ring):
        summed = summed + stats[i]
    gain_out[...] = summed[0:1]
    scale_out[...] = summed[1:2]

    for way, hops in ((0, hops_a), (1, hops_b)):
        for step in range(hops):
            for buffer, rows, sems, own in weights:
                gather_copy(
                    buffer, rows, sems, way, step, own if step == 0 else None
                ).wait_send()
            rs_copy(way, step).wait_send()
            stat_copy(way, step).wait_send()

    for p in range(PIECES):
        for c in range(CHUNKS):
            chain_copy(p, c).wait_send()

    @pl.when(s == last)
    def _():
        for p in range(PIECES):
            for c in range(CHUNKS):
                chain_arrival(p, c, 1).wait_recv()


def shards(stages, ring, x_saved, up_weights, down_weights, norm_gain, layer_scale, cotangent, lengths):
    unused, rows, width = x_saved.shape
    ff = up_weights.shape[2]
    down_rows = down_weights.shape[1]
    tokens = rows * 5 // 8
    hops_a = ring // 2
    hops_b = ring - 1 - hops_a
    vmem = pl.BlockSpec(memory_space=pltpu.VMEM)
    smem = pl.BlockSpec(memory_space=pltpu.SMEM)
    return pl.pallas_call(
        functools.partial(kernel, stages, ring),
        out_shape=(
            jax.ShapeDtypeStruct((1, down_rows, width), BF16),
            jax.ShapeDtypeStruct((1, width), F32),
            jax.ShapeDtypeStruct((1, width), F32),
        ),
        in_specs=[smem] + [vmem] * 6,
        out_specs=(vmem, vmem, vmem),
        scratch_shapes=[
            pltpu.VMEM((width, ff), BF16),
            pltpu.VMEM((ff, width), BF16),
            pltpu.VMEM((ff, width), BF16),
            pltpu.VMEM((width, ff), BF16),
            pltpu.VMEM((tokens, ff), F32),
            pltpu.VMEM((tokens, ff), F32),
            pltpu.VMEM((tokens, ff), BF16),
            pltpu.VMEM((ff, tokens), BF16),
            pltpu.VMEM((tokens, width), F32),
            pltpu.VMEM((tokens, 128), F32),
            pltpu.VMEM((tokens, width), BF16),
            pltpu.VMEM((tokens, width), F32),
            pltpu.VMEM((tokens, width), BF16),
            pltpu.VMEM((2, CHUNKS, tokens, width // CHUNKS), BF16),
            pltpu.VMEM((CHUNKS, tokens, width // CHUNKS), BF16),
            pltpu.VMEM((tokens, width), BF16),
            pltpu.VMEM((tokens, ff), BF16),
            pltpu.VMEM((1, width), F32),
            pltpu.VMEM((ring, 2, width), F32),
            pltpu.VMEM((hops_a, down_rows, width), BF16),
            pltpu.VMEM((hops_a, down_rows, width), BF16),
            pltpu.VMEM((hops_b, down_rows, width), BF16),
            pltpu.VMEM((hops_b, down_rows, width), BF16),
            pltpu.SemaphoreType.DMA((2, 2, hops_a)),
            pltpu.SemaphoreType.DMA((2, 2, hops_a)),
            pltpu.SemaphoreType.DMA((2, PIECES, CHUNKS)),
            pltpu.SemaphoreType.DMA((2, 2, hops_a)),
            pltpu.SemaphoreType.DMA((2, 2, hops_a)),
        ],
        compiler_params=pltpu.CompilerParams(
            collective_id=0,
            has_side_effects=True,
            vmem_limit_bytes=60 * 1024 * 1024,
        ),
        name="layer_chain",
    )(lengths, up_weights, down_weights, x_saved, cotangent, norm_gain, layer_scale)


def solution(mesh):
    return jax.shard_map(
        functools.partial(shards, mesh.shape["pipe"], mesh.shape["dp"]),
        mesh=mesh,
        in_specs=(
            P("pipe", "dp", None),
            P("pipe", "dp", None),
            P("pipe", "dp", None),
            P("pipe", None),
            P("pipe", None),
            P("dp", None),
            P("dp", None),
        ),
        out_specs=(P("pipe", "dp", None), P("pipe", None), P("pipe", None)),
        check_vma=False,
    )
```

```python
import functools

import jax
import jax.numpy as jnp
from jax import lax
from jax.experimental import pallas as pl
from jax.experimental.pallas import tpu as pltpu
from jax.sharding import PartitionSpec as P

EPSILON = 1e-06
ROOT = 0.7978845608028654
CUBIC = 0.044715
PIECES = 5
CHUNKS = 2
F_TILE = 512
LAG = 2
MESH = pl.DeviceIdType.MESH
F32 = jnp.float32
BF16 = jnp.bfloat16


def kernel(
    stages,
    ring,
    len_ref,
    up_ref,
    down_ref,
    x_ref,
    cot_ref,
    gain_ref,
    scale_ref,
    out_ref,
    gain_out,
    scale_out,
    up_w,
    down_w,
    up_t,
    down_t,
    hidden,
    slope,
    act,
    act_t,
    unit,
    inverse,
    normed,
    branch,
    start,
    g_in,
    back,
    bg,
    hg,
    gain_acc,
    stats,
    rs_send_a,
    rs_recv_a,
    rs_send_b,
    rs_recv_b,
    help_up,
    help_down,
    rest_in_a,
    rest_in_b,
    rest_send_a,
    rest_send_b,
    rest_recv_a,
    rest_recv_b,
    rest_out,
    rest_back,
    ag_sems,
    help_sems,
    seed_sems,
    chain_sems,
    rs_sems,
    rest_sems,
    rest_ring_sems,
    back_sems,
    stat_sems,
):
    s = lax.axis_index("pipe")
    z = lax.axis_index("dp")
    last = stages - 1
    right = lax.rem(z + 1, ring)
    left = lax.rem(z + ring - 1, ring)
    above = lax.rem(s + 1, stages)
    below = lax.rem(s + stages - 1, stages)
    width, ff = up_w.shape
    up_rows = up_ref.shape[1]
    down_rows = down_ref.shape[1]
    tokens = normed.shape[0]
    slot = x_ref.shape[1] // 2
    hops_a = ring // 2
    hops_b = ring - 1 - hops_a
    piece_rows = tokens // PIECES
    chunk = width // CHUNKS

    barrier = pltpu.get_barrier_semaphore()
    quarter = stages // 4
    partner = lax.rem(s + quarter, stages)
    other = lax.rem(s + stages - quarter, stages)
    for place in (
        {"dp": right},
        {"dp": left},
        {"pipe": above},
        {"pipe": below},
        {"pipe": partner},
        {"pipe": other},
    ):
        pl.semaphore_signal(barrier, inc=1, device_id=place, device_id_type=MESH)
    pl.semaphore_wait(barrier, 6)
    early = s >= stages - quarter
    late = s < quarter

    up_rest = up_rows // 4
    down_rest = down_rows * 3 // 8
    ways = ((0, hops_a), (1, hops_b))
    weights = (
        (up_w, up_rows, up_rest, up_ref, help_up),
        (down_w, down_rows, down_rest, down_ref, help_down),
    )

    def owner_at(way, distance):
        if way == 0:
            return lax.rem(z - distance + ring, ring)
        return lax.rem(z + distance, ring)

    def target_of(way):
        return {"dp": right if way == 0 else left}

    def block_of(kind, part, owner):
        buffer, rows, rest, own, helper = weights[kind]
        first, size = (0, rows - rest) if part == 0 else (rows - rest, rest)
        return buffer.at[pl.ds(pl.multiple_of(owner * rows + first, 16), size)]

    def own_block(kind, part):
        buffer, rows, rest, own, helper = weights[kind]
        first, size = (0, rows - rest) if part == 0 else (rows - rest, rest)
        return own.at[0, pl.ds(first, size)]

    def gather_copy(kind, part, way, step, arrival=False):
        block = block_of(kind, part, owner_at(way, step + 1 if arrival else step))
        return pltpu.make_async_remote_copy(
            src_ref=own_block(kind, part) if step == 0 and not arrival else block,
            dst_ref=block,
            send_sem=ag_sems.at[0, kind, part, way, step],
            recv_sem=ag_sems.at[1, kind, part, way, step],
            device_id=target_of(way),
            device_id_type=MESH,
        )

    def gather_part(kind, part, step):
        for way, hops in ways:
            if step > 0 and step <= hops:
                gather_copy(kind, part, way, step - 1, True).wait_recv()
            if step < hops:
                gather_copy(kind, part, way, step).start()

    def gather_step(kind, step):
        gather_part(kind, 0, step)

        @pl.when(jnp.logical_not(early))
        def _():
            gather_part(kind, 1, step)

    def rest_arrivals(kind, steps):
        @pl.when(early)
        def _():
            for step in steps:
                for way, hops in ways:
                    if step > 0 and step <= hops:
                        gather_copy(kind, 1, way, step - 1, True).wait_recv()

    def help_block(kind, owner):
        buffer, rows, rest, own, helper = weights[kind]
        return helper.at[pl.ds(pl.multiple_of(owner * rest, 16), rest)]

    def seed_copy(kind):
        return pltpu.make_async_remote_copy(
            src_ref=own_block(kind, 1),
            dst_ref=help_block(kind, z),
            send_sem=seed_sems.at[0, kind],
            recv_sem=seed_sems.at[1, kind],
            device_id={"pipe": partner},
            device_id_type=MESH,
        )

    def help_copy(kind, way, step, arrival=False):
        block = help_block(kind, owner_at(way, step + 1 if arrival else step))
        return pltpu.make_async_remote_copy(
            src_ref=block,
            dst_ref=block,
            send_sem=help_sems.at[0, kind, way, step],
            recv_sem=help_sems.at[1, kind, way, step],
            device_id=target_of(way),
            device_id_type=MESH,
        )

    def forward_copy(kind, way, step):
        owner = owner_at(way, step + 1)
        return pltpu.make_async_remote_copy(
            src_ref=help_block(kind, owner),
            dst_ref=block_of(kind, 1, owner),
            send_sem=help_sems.at[2, kind, way, step],
            recv_sem=ag_sems.at[1, kind, 1, way, step],
            device_id={"pipe": other},
            device_id_type=MESH,
        )

    @pl.when(early)
    def _():
        for kind in range(2):
            seed_copy(kind).start()

    @pl.when(late)
    def _():
        for kind in range(2):
            seed_copy(kind).wait_recv()
        for step in range(hops_a + 1):
            for kind in range(2):
                for way, hops in ways:
                    if step > 0 and step <= hops:
                        help_copy(kind, way, step - 1, True).wait_recv()
                    if step < hops:
                        help_copy(kind, way, step).start()
                    if step > 0 and step <= hops:
                        forward_copy(kind, way, step - 1).start()

    gather_step(0, 0)
    for buffer, rows, rest, own, helper in weights:
        buffer[pl.ds(pl.multiple_of(z * rows, rows), rows)] = own[0]

    first_len = len_ref[0, 0]
    row = lax.broadcasted_iota(jnp.int32, (tokens, x_ref.shape[1]), 0)
    col = lax.broadcasted_iota(jnp.int32, (tokens, x_ref.shape[1]), 1)
    source = jnp.where(row < first_len, row, row + (slot - first_len))
    pick = (col == source).astype(F32).astype(BF16)
    x_rows = jnp.dot(pick, x_ref[0], preferred_element_type=F32)
    scaled = lax.rsqrt(jnp.mean(x_rows * x_rows, axis=-1, keepdims=True) + EPSILON)
    inverse[...] = jnp.broadcast_to(scaled, inverse.shape)
    unit_rows = x_rows * scaled
    unit[...] = unit_rows
    normed[...] = (unit_rows * gain_ref[...]).astype(BF16)
    start[...] = jnp.dot(pick, cot_ref[...], preferred_element_type=F32).astype(BF16)
    gain_acc[...] = jnp.zeros_like(gain_acc)

    def hidden_tile(tile):
        cols = pl.ds(pl.multiple_of(tile * F_TILE, F_TILE), F_TILE)
        h = jnp.dot(normed[...], up_w[:, cols], preferred_element_type=F32)
        square = h * h
        th = jnp.tanh(ROOT * (h + CUBIC * (square * h)))
        half = 0.5 * (1.0 + th)
        a = h * half
        hidden[:, cols] = h
        slope[:, cols] = half + 0.5 * h * (1.0 - th * th) * (
            ROOT * (1.0 + (3.0 * CUBIC) * square)
        )
        act[:, cols] = a.astype(BF16)
        act_t[cols, :] = a.T.astype(BF16)

    def turn_up(block, carry):
        rows = pl.ds(pl.multiple_of(block * 128, 128), 128)
        up_t[:, rows] = up_w[rows, :].T
        return carry

    def turn_down(owner):
        for part in range(down_rows // 128):
            rows = pl.ds(pl.multiple_of(owner * down_rows + part * 128, 128), 128)
            down_t[:, rows] = down_w[rows, :].T

    turn_down(z)
    blocks = width // 128
    tiles = ff // F_TILE
    for step in range(1, hops_a + LAG + 1):
        if step <= hops_a:
            gather_step(0, step)
        if step == hops_a:
            rest_arrivals(0, range(1, hops_a + 1))
        if step >= LAG:
            gather_step(1, step - LAG)
            done = step - LAG
            rest_arrivals(1, (done,))
            if done > 0 and done <= hops_a:
                turn_down(lax.rem(z - done + ring, ring))
            if done > 0 and done <= hops_b:
                turn_down(lax.rem(z + done, ring))
        if step >= hops_a and step < hops_a + LAG:
            part = step - hops_a
            lax.fori_loop(
                part * tiles // LAG,
                (part + 1) * tiles // LAG,
                lambda tile, c: (hidden_tile(tile), c)[1],
                0,
            )
            lax.fori_loop(part * blocks // LAG, (part + 1) * blocks // LAG, turn_up, 0)

    @pl.when(s == last)
    def _():
        for c in range(CHUNKS):
            g_in[0, c] = start[:, c * chunk : (c + 1) * chunk]

    def branch_tile(tile, carry):
        cols = pl.ds(pl.multiple_of(tile * F_TILE, F_TILE), F_TILE)
        branch[:, cols] = jnp.dot(act[...], down_w[:, cols], preferred_element_type=F32)
        return carry

    @pl.when(s < last)
    def _():
        lax.fori_loop(0, width // F_TILE, branch_tile, 0)

    landing = jnp.where(s == 0, 1, 0)

    def chain_copy(p, c):
        rows = pl.ds(pl.multiple_of(p * piece_rows, piece_rows), piece_rows)
        return pltpu.make_async_remote_copy(
            src_ref=back.at[c, rows],
            dst_ref=g_in.at[landing, c, rows],
            send_sem=chain_sems.at[0, p, c],
            recv_sem=chain_sems.at[1, p, c],
            device_id={"pipe": below},
            device_id_type=MESH,
        )

    def chain_arrival(p, c, slot):
        rows = pl.ds(pl.multiple_of(p * piece_rows, piece_rows), piece_rows)
        return pltpu.make_async_remote_copy(
            src_ref=back.at[c, rows],
            dst_ref=g_in.at[slot, c, rows],
            send_sem=chain_sems.at[0, p, c],
            recv_sem=chain_sems.at[1, p, c],
            device_id={"pipe": below},
            device_id_type=MESH,
        )

    def piece(p, carry):
        rows = pl.ds(pl.multiple_of(p * piece_rows, piece_rows), piece_rows)

        @pl.when(s < last)
        def _():
            for c in range(CHUNKS):
                chain_arrival(p, c, 0).wait_recv()

        for c in range(CHUNKS):
            cols = slice(c * chunk, (c + 1) * chunk)
            bg[rows, cols] = (g_in[0, c, rows].astype(F32) * scale_ref[:, cols]).astype(BF16)
        grad = bg[rows, :]
        total = jnp.zeros((piece_rows, 1), F32)
        for f in range(tiles):
            cols = slice(f * F_TILE, (f + 1) * F_TILE)
            act_grad = jnp.dot(grad, down_t[:, cols], preferred_element_type=F32)
            rounded = (act_grad * slope[rows, cols]).astype(BF16)
            hg[rows, cols] = rounded
            total += jnp.sum(rounded.astype(F32) * hidden[rows, cols], axis=-1, keepdims=True)
        mean = total * (1.0 / width)
        inv = inverse[rows, 0:1]
        hidden_grad = hg[rows, :]
        for c in range(CHUNKS):
            cols = slice(c * chunk, (c + 1) * chunk)
            normed_grad = jnp.dot(hidden_grad, up_t[:, cols], preferred_element_type=F32)
            unit_part = unit[rows, cols]
            back[c, rows] = (
                g_in[0, c, rows].astype(F32)
                + inv * (normed_grad * gain_ref[:, cols] - unit_part * mean)
            ).astype(BF16)
            chain_copy(p, c).start()
            gain_acc[:, cols] += jnp.sum(normed_grad * unit_part, axis=0, keepdims=True)
        return carry

    lax.fori_loop(0, PIECES, piece, 0)

    @pl.when(s == last)
    def _():
        lax.fori_loop(0, width // F_TILE, branch_tile, 0)

    stats[z, 0:1, :] = gain_acc[...]
    for c in range(CHUNKS):
        cols = slice(c * chunk, (c + 1) * chunk)
        stats[z, 1:2, cols] = jnp.sum(
            g_in[0, c].astype(F32) * branch[:, cols], axis=0, keepdims=True
        )

    rest = down_rows // 4
    main = down_rows - rest
    half = width // 2
    slots = (
        (rs_send_a, rs_recv_a, rest_in_a, rest_send_a, rest_recv_a),
        (rs_send_b, rs_recv_b, rest_in_b, rest_send_b, rest_recv_b),
    )

    def own_part(dest, first, size, cols):
        rows = pl.ds(pl.multiple_of(dest * down_rows + first, 32), size)
        return jnp.dot(act_t[rows, :], bg[:, cols], preferred_element_type=F32)

    def rs_copy(way, part, j):
        sent, received = slots[way][:2]
        rows = pl.ds(0, main) if part == 0 else pl.ds(main, rest)
        return pltpu.make_async_remote_copy(
            src_ref=sent.at[j, rows],
            dst_ref=received.at[j, rows],
            send_sem=rs_sems.at[0, part, way, j],
            recv_sem=rs_sems.at[1, part, way, j],
            device_id=target_of(way),
            device_id_type=MESH,
        )

    def rest_copy(way, j):
        return pltpu.make_async_remote_copy(
            src_ref=slots[way][0].at[j, pl.ds(main, rest)],
            dst_ref=slots[way][2].at[j],
            send_sem=rest_sems.at[0, way, j],
            recv_sem=rest_sems.at[1, way, j],
            device_id={"pipe": other},
            device_id_type=MESH,
        )

    def rest_ring_copy(way, j):
        return pltpu.make_async_remote_copy(
            src_ref=slots[way][2].at[0] if j == 0 else slots[way][3].at[j],
            dst_ref=slots[way][4].at[j],
            send_sem=rest_ring_sems.at[0, way, j],
            recv_sem=rest_ring_sems.at[1, way, j],
            device_id=target_of(way),
            device_id_type=MESH,
        )

    def back_copy():
        return pltpu.make_async_remote_copy(
            src_ref=rest_out,
            dst_ref=rest_back,
            send_sem=back_sems.at[0],
            recv_sem=back_sems.at[1],
            device_id={"pipe": partner},
            device_id_type=MESH,
        )

    def stat_copy(way, j, arrival=False):
        ahead = j + 1 if arrival else j
        owner = lax.rem(z - ahead + ring, ring) if way == 0 else lax.rem(z + ahead, ring)
        return pltpu.make_async_remote_copy(
            src_ref=stats.at[owner],
            dst_ref=stats.at[owner],
            send_sem=stat_sems.at[0, way, j],
            recv_sem=stat_sems.at[1, way, j],
            device_id={"dp": right if way == 0 else left},
            device_id_type=MESH,
        )

    def rs_part(way, part, j, dest, add):
        sent, received = slots[way][:2]
        first, size = (0, main) if part == 0 else (main, rest)
        for cols in (slice(0, half), slice(half, width)):
            value = own_part(dest, first, size, cols)
            if add:
                value = value + received[j - 1, first : first + size, cols].astype(F32)
            sent[j, first : first + size, cols] = value.astype(BF16)

    def rs_step(j, carry):
        for way, hops in ways:

            @pl.when(j < hops)
            def _():
                dest = owner_at(1 - way, hops - j)

                @pl.when(late)
                def _():
                    rs_part(way, 1, j, dest, False)
                    rest_copy(way, j).start()

                @pl.when(j == 0)
                def _():
                    rs_part(way, 0, j, dest, False)

                @pl.when(j > 0)
                def _():
                    rs_copy(way, 0, j - 1).wait_recv()
                    rs_part(way, 0, j, dest, True)

                rs_copy(way, 0, j).start()

                @pl.when(jnp.logical_and(jnp.logical_not(late), j == 0))
                def _():
                    rs_part(way, 1, j, dest, False)
                    rs_copy(way, 1, j).start()

                @pl.when(jnp.logical_and(jnp.logical_not(late), j > 0))
                def _():
                    rs_copy(way, 1, j - 1).wait_recv()
                    rs_part(way, 1, j, dest, True)
                    rs_copy(way, 1, j).start()

                @pl.when(j > 0)
                def _():
                    stat_copy(way, j - 1, True).wait_recv()

                stat_copy(way, j).start()

        return carry

    lax.fori_loop(0, hops_a, rs_step, 0)

    @pl.when(early)
    def _():
        for j in range(hops_a):
            for way, hops in ways:
                if j < hops:
                    rest_copy(way, j).wait_recv()
                    if j > 0:
                        rest_ring_copy(way, j - 1).wait_recv()
                        slots[way][3][j] = (
                            slots[way][2][j].astype(F32) + slots[way][4][j - 1].astype(F32)
                        ).astype(BF16)
                    rest_ring_copy(way, j).start()
        total = jnp.zeros((rest, width), F32)
        for way, hops in ways:
            rest_ring_copy(way, hops - 1).wait_recv()
            total = total + slots[way][4][hops - 1].astype(F32)
        rest_out[...] = total.astype(BF16)
        back_copy().start()

    for way, hops in ways:
        rs_copy(way, 0, hops - 1).wait_recv()
        stat_copy(way, hops - 1, True).wait_recv()
    for cols in (slice(0, half), slice(half, width)):
        value = own_part(z, 0, main, cols)
        for way, hops in ways:
            value = value + slots[way][1][hops - 1, 0:main, cols].astype(F32)
        out_ref[0, 0:main, cols] = value.astype(BF16)

    @pl.when(late)
    def _():
        back_copy().wait_recv()
        for cols in (slice(0, half), slice(half, width)):
            value = own_part(z, main, rest, cols) + rest_back[:, cols].astype(F32)
            out_ref[0, main:, cols] = value.astype(BF16)

    @pl.when(jnp.logical_not(late))
    def _():
        for way, hops in ways:
            rs_copy(way, 1, hops - 1).wait_recv()
        for cols in (slice(0, half), slice(half, width)):
            value = own_part(z, main, rest, cols)
            for way, hops in ways:
                value = value + slots[way][1][hops - 1, main:, cols].astype(F32)
            out_ref[0, main:, cols] = value.astype(BF16)

    summed = stats[0]
    for i in range(1, ring):
        summed = summed + stats[i]
    gain_out[...] = summed[0:1]
    scale_out[...] = summed[1:2]

    for way, hops in ways:
        for step in range(hops):
            for kind in range(2):
                gather_copy(kind, 0, way, step).wait_send()
            rs_copy(way, 0, step).wait_send()
            stat_copy(way, step).wait_send()

    @pl.when(jnp.logical_not(early))
    def _():
        for way, hops in ways:
            for step in range(hops):
                for kind in range(2):
                    gather_copy(kind, 1, way, step).wait_send()

    @pl.when(jnp.logical_not(late))
    def _():
        for way, hops in ways:
            for step in range(hops):
                rs_copy(way, 1, step).wait_send()

    @pl.when(early)
    def _():
        for kind in range(2):
            seed_copy(kind).wait_send()
        for way, hops in ways:
            for step in range(hops):
                rest_ring_copy(way, step).wait_send()
        back_copy().wait_send()

    @pl.when(late)
    def _():
        for way, hops in ways:
            for step in range(hops):
                for kind in range(2):
                    help_copy(kind, way, step).wait_send()
                    forward_copy(kind, way, step).wait_send()
                rest_copy(way, step).wait_send()

    for p in range(PIECES):
        for c in range(CHUNKS):
            chain_copy(p, c).wait_send()

    @pl.when(s == last)
    def _():
        for p in range(PIECES):
            for c in range(CHUNKS):
                chain_arrival(p, c, 1).wait_recv()


def shards(stages, ring, x_saved, up_weights, down_weights, norm_gain, layer_scale, cotangent, lengths):
    unused, rows, width = x_saved.shape
    ff = up_weights.shape[2]
    down_rows = down_weights.shape[1]
    tokens = rows * 5 // 8
    hops_a = ring // 2
    hops_b = ring - 1 - hops_a
    vmem = pl.BlockSpec(memory_space=pltpu.VMEM)
    smem = pl.BlockSpec(memory_space=pltpu.SMEM)
    return pl.pallas_call(
        functools.partial(kernel, stages, ring),
        out_shape=(
            jax.ShapeDtypeStruct((1, down_rows, width), BF16),
            jax.ShapeDtypeStruct((1, width), F32),
            jax.ShapeDtypeStruct((1, width), F32),
        ),
        in_specs=[smem] + [vmem] * 6,
        out_specs=(vmem, vmem, vmem),
        scratch_shapes=[
            pltpu.VMEM((width, ff), BF16),
            pltpu.VMEM((ff, width), BF16),
            pltpu.VMEM((ff, width), BF16),
            pltpu.VMEM((width, ff), BF16),
            pltpu.VMEM((tokens, ff), F32),
            pltpu.VMEM((tokens, ff), F32),
            pltpu.VMEM((tokens, ff), BF16),
            pltpu.VMEM((ff, tokens), BF16),
            pltpu.VMEM((tokens, width), F32),
            pltpu.VMEM((tokens, 128), F32),
            pltpu.VMEM((tokens, width), BF16),
            pltpu.VMEM((tokens, width), F32),
            pltpu.VMEM((tokens, width), BF16),
            pltpu.VMEM((2, CHUNKS, tokens, width // CHUNKS), BF16),
            pltpu.VMEM((CHUNKS, tokens, width // CHUNKS), BF16),
            pltpu.VMEM((tokens, width), BF16),
            pltpu.VMEM((tokens, ff), BF16),
            pltpu.VMEM((1, width), F32),
            pltpu.VMEM((ring, 2, width), F32),
            pltpu.VMEM((hops_a, down_rows, width), BF16),
            pltpu.VMEM((hops_a, down_rows, width), BF16),
            pltpu.VMEM((hops_b, down_rows, width), BF16),
            pltpu.VMEM((hops_b, down_rows, width), BF16),
            pltpu.VMEM((width // 4, ff), BF16),
            pltpu.VMEM((ff * 3 // 8, width), BF16),
            pltpu.VMEM((hops_a, down_rows // 4, width), BF16),
            pltpu.VMEM((hops_b, down_rows // 4, width), BF16),
            pltpu.VMEM((hops_a, down_rows // 4, width), BF16),
            pltpu.VMEM((hops_b, down_rows // 4, width), BF16),
            pltpu.VMEM((hops_a, down_rows // 4, width), BF16),
            pltpu.VMEM((hops_b, down_rows // 4, width), BF16),
            pltpu.VMEM((down_rows // 4, width), BF16),
            pltpu.VMEM((down_rows // 4, width), BF16),
            pltpu.SemaphoreType.DMA((2, 2, 2, 2, hops_a)),
            pltpu.SemaphoreType.DMA((3, 2, 2, hops_a)),
            pltpu.SemaphoreType.DMA((2, 2)),
            pltpu.SemaphoreType.DMA((2, PIECES, CHUNKS)),
            pltpu.SemaphoreType.DMA((2, 2, 2, hops_a)),
            pltpu.SemaphoreType.DMA((2, 2, hops_a)),
            pltpu.SemaphoreType.DMA((2, 2, hops_a)),
            pltpu.SemaphoreType.DMA((2,)),
            pltpu.SemaphoreType.DMA((2, 2, hops_a)),
        ],
        compiler_params=pltpu.CompilerParams(
            collective_id=0,
            has_side_effects=True,
            vmem_limit_bytes=60 * 1024 * 1024,
        ),
        name="layer_chain",
    )(lengths, up_weights, down_weights, x_saved, cotangent, norm_gain, layer_scale)


def solution(mesh):
    return jax.shard_map(
        functools.partial(shards, mesh.shape["pipe"], mesh.shape["dp"]),
        mesh=mesh,
        in_specs=(
            P("pipe", "dp", None),
            P("pipe", "dp", None),
            P("pipe", "dp", None),
            P("pipe", None),
            P("pipe", None),
            P("dp", None),
            P("dp", None),
        ),
        out_specs=(P("pipe", "dp", None), P("pipe", None), P("pipe", None)),
        check_vma=False,
    )
```

```python
import functools

import jax
import jax.numpy as jnp
from jax import lax
from jax.experimental import pallas as pl
from jax.experimental.pallas import tpu as pltpu
from jax.sharding import PartitionSpec as P

EPSILON = 1e-06
ROOT = 0.7978845608028654
CUBIC = 0.044715
PIECES = 5
CHUNKS = 2
F_TILE = 512
LAG = 2
MESH = pl.DeviceIdType.MESH
F32 = jnp.float32
BF16 = jnp.bfloat16


def kernel(
    stages,
    ring,
    len_ref,
    up_ref,
    down_ref,
    x_ref,
    cot_ref,
    gain_ref,
    scale_ref,
    out_ref,
    gain_out,
    scale_out,
    up_w,
    down_w,
    up_t,
    down_t,
    hidden,
    slope,
    act,
    act_t,
    unit,
    inverse,
    normed,
    branch,
    start,
    g_in,
    back,
    bg,
    hg,
    gain_acc,
    partial,
    stats,
    rs_send_a,
    rs_recv_a,
    rs_send_b,
    rs_recv_b,
    rest_own_a,
    rest_own_b,
    own_sum,
    help_up,
    help_down,
    rest_in_a,
    rest_in_b,
    rest_send_a,
    rest_send_b,
    rest_recv_a,
    rest_recv_b,
    rest_out,
    rest_back,
    ag_sems,
    help_sems,
    seed_sems,
    chain_sems,
    rs_sems,
    rest_sems,
    rest_ring_sems,
    back_sems,
    stat_sems,
):
    s = lax.axis_index("pipe")
    z = lax.axis_index("dp")
    last = stages - 1
    right = lax.rem(z + 1, ring)
    left = lax.rem(z + ring - 1, ring)
    above = lax.rem(s + 1, stages)
    below = lax.rem(s + stages - 1, stages)
    width, ff = up_w.shape
    up_rows = up_ref.shape[1]
    down_rows = down_ref.shape[1]
    tokens = normed.shape[0]
    slot = x_ref.shape[1] // 2
    hops_a = ring // 2
    hops_b = ring - 1 - hops_a
    piece_rows = tokens // PIECES
    chunk = width // CHUNKS

    barrier = pltpu.get_barrier_semaphore()
    quarter = stages // 4
    partner = lax.rem(s + quarter, stages)
    other = lax.rem(s + stages - quarter, stages)
    for place in (
        {"dp": right},
        {"dp": left},
        {"pipe": above},
        {"pipe": below},
        {"pipe": partner},
        {"pipe": other},
    ):
        pl.semaphore_signal(barrier, inc=1, device_id=place, device_id_type=MESH)
    pl.semaphore_wait(barrier, 6)
    early = s >= stages - quarter
    late = s < quarter

    up_rest = up_rows // 4
    down_rest = down_rows * 3 // 8
    ways = ((0, hops_a), (1, hops_b))
    weights = (
        (up_w, up_rows, up_rest, up_ref, help_up),
        (down_w, down_rows, down_rest, down_ref, help_down),
    )

    def owner_at(way, distance):
        if way == 0:
            return lax.rem(z - distance + ring, ring)
        return lax.rem(z + distance, ring)

    def target_of(way):
        return {"dp": right if way == 0 else left}

    def block_of(kind, part, owner):
        buffer, rows, rest, own, helper = weights[kind]
        first, size = (0, rows - rest) if part == 0 else (rows - rest, rest)
        return buffer.at[pl.ds(pl.multiple_of(owner * rows + first, 16), size)]

    def own_block(kind, part):
        buffer, rows, rest, own, helper = weights[kind]
        first, size = (0, rows - rest) if part == 0 else (rows - rest, rest)
        return own.at[0, pl.ds(first, size)]

    def gather_copy(kind, part, way, step, arrival=False):
        block = block_of(kind, part, owner_at(way, step + 1 if arrival else step))
        return pltpu.make_async_remote_copy(
            src_ref=own_block(kind, part) if step == 0 and not arrival else block,
            dst_ref=block,
            send_sem=ag_sems.at[0, kind, part, way, step],
            recv_sem=ag_sems.at[1, kind, part, way, step],
            device_id=target_of(way),
            device_id_type=MESH,
        )

    def gather_part(kind, part, step):
        for way, hops in ways:
            if step > 0 and step <= hops:
                gather_copy(kind, part, way, step - 1, True).wait_recv()
            if step < hops:
                gather_copy(kind, part, way, step).start()

    def gather_step(kind, step):
        gather_part(kind, 0, step)

        @pl.when(jnp.logical_not(early))
        def _():
            gather_part(kind, 1, step)

    def rest_arrivals(kind, steps):
        @pl.when(early)
        def _():
            for step in steps:
                for way, hops in ways:
                    if step > 0 and step <= hops:
                        gather_copy(kind, 1, way, step - 1, True).wait_recv()

    def help_block(kind, owner):
        buffer, rows, rest, own, helper = weights[kind]
        return helper.at[pl.ds(pl.multiple_of(owner * rest, 16), rest)]

    def seed_copy(kind):
        return pltpu.make_async_remote_copy(
            src_ref=own_block(kind, 1),
            dst_ref=help_block(kind, z),
            send_sem=seed_sems.at[0, kind],
            recv_sem=seed_sems.at[1, kind],
            device_id={"pipe": partner},
            device_id_type=MESH,
        )

    def help_copy(kind, way, step, arrival=False):
        block = help_block(kind, owner_at(way, step + 1 if arrival else step))
        return pltpu.make_async_remote_copy(
            src_ref=block,
            dst_ref=block,
            send_sem=help_sems.at[0, kind, way, step],
            recv_sem=help_sems.at[1, kind, way, step],
            device_id=target_of(way),
            device_id_type=MESH,
        )

    def forward_copy(kind, way, step):
        owner = owner_at(way, step + 1)
        return pltpu.make_async_remote_copy(
            src_ref=help_block(kind, owner),
            dst_ref=block_of(kind, 1, owner),
            send_sem=help_sems.at[2, kind, way, step],
            recv_sem=ag_sems.at[1, kind, 1, way, step],
            device_id={"pipe": other},
            device_id_type=MESH,
        )

    @pl.when(early)
    def _():
        for kind in range(2):
            seed_copy(kind).start()

    @pl.when(late)
    def _():
        for kind in range(2):
            seed_copy(kind).wait_recv()
        for step in range(hops_a + 1):
            for kind in range(2):
                for way, hops in ways:
                    if step > 0 and step <= hops:
                        help_copy(kind, way, step - 1, True).wait_recv()
                    if step < hops:
                        help_copy(kind, way, step).start()
                    if step > 0 and step <= hops:
                        forward_copy(kind, way, step - 1).start()

    gather_step(0, 0)
    for buffer, rows, rest, own, helper in weights:
        buffer[pl.ds(pl.multiple_of(z * rows, rows), rows)] = own[0]

    first_len = len_ref[0, 0]
    row = lax.broadcasted_iota(jnp.int32, (tokens, x_ref.shape[1]), 0)
    col = lax.broadcasted_iota(jnp.int32, (tokens, x_ref.shape[1]), 1)
    source = jnp.where(row < first_len, row, row + (slot - first_len))
    pick = (col == source).astype(F32).astype(BF16)
    x_rows = jnp.dot(pick, x_ref[0], preferred_element_type=F32)
    scaled = lax.rsqrt(jnp.mean(x_rows * x_rows, axis=-1, keepdims=True) + EPSILON)
    inverse[...] = jnp.broadcast_to(scaled, inverse.shape)
    unit_rows = x_rows * scaled
    unit[...] = unit_rows
    normed[...] = (unit_rows * gain_ref[...]).astype(BF16)
    start[...] = jnp.dot(pick, cot_ref[...], preferred_element_type=F32).astype(BF16)
    gain_acc[...] = jnp.zeros_like(gain_acc)

    def hidden_tile(tile):
        cols = pl.ds(pl.multiple_of(tile * F_TILE, F_TILE), F_TILE)
        h = jnp.dot(normed[...], up_w[:, cols], preferred_element_type=F32)
        square = h * h
        th = jnp.tanh(ROOT * (h + CUBIC * (square * h)))
        half = 0.5 * (1.0 + th)
        a = h * half
        hidden[:, cols] = h
        slope[:, cols] = half + 0.5 * h * (1.0 - th * th) * (
            ROOT * (1.0 + (3.0 * CUBIC) * square)
        )
        act[:, cols] = a.astype(BF16)
        act_t[cols, :] = a.T.astype(BF16)

    def turn_up(block, carry):
        rows = pl.ds(pl.multiple_of(block * 128, 128), 128)
        up_t[:, rows] = up_w[rows, :].T
        return carry

    def turn_down(owner):
        for part in range(down_rows // 128):
            rows = pl.ds(pl.multiple_of(owner * down_rows + part * 128, 128), 128)
            down_t[:, rows] = down_w[rows, :].T

    turn_down(z)
    blocks = width // 128
    tiles = ff // F_TILE
    for step in range(1, hops_a + LAG + 1):
        if step <= hops_a:
            gather_step(0, step)
        if step == hops_a:
            rest_arrivals(0, range(1, hops_a + 1))
        if step >= LAG:
            gather_step(1, step - LAG)
            done = step - LAG
            rest_arrivals(1, (done,))
            if done > 0 and done <= hops_a:
                turn_down(lax.rem(z - done + ring, ring))
            if done > 0 and done <= hops_b:
                turn_down(lax.rem(z + done, ring))
        if step >= hops_a and step < hops_a + LAG:
            part = step - hops_a
            lax.fori_loop(
                part * tiles // LAG,
                (part + 1) * tiles // LAG,
                lambda tile, c: (hidden_tile(tile), c)[1],
                0,
            )
            lax.fori_loop(part * blocks // LAG, (part + 1) * blocks // LAG, turn_up, 0)

    @pl.when(s == last)
    def _():
        for c in range(CHUNKS):
            g_in[0, c] = start[:, c * chunk : (c + 1) * chunk]

    def branch_tile(tile, carry):
        cols = pl.ds(pl.multiple_of(tile * F_TILE, F_TILE), F_TILE)
        branch[:, cols] = jnp.dot(act[...], down_w[:, cols], preferred_element_type=F32)
        return carry

    @pl.when(jnp.logical_not(early))
    def _():
        lax.fori_loop(0, width // F_TILE, branch_tile, 0)

    landing = jnp.where(s == 0, 1, 0)

    def chain_copy(p, c):
        rows = pl.ds(pl.multiple_of(p * piece_rows, piece_rows), piece_rows)
        return pltpu.make_async_remote_copy(
            src_ref=back.at[c, rows],
            dst_ref=g_in.at[landing, c, rows],
            send_sem=chain_sems.at[0, p, c],
            recv_sem=chain_sems.at[1, p, c],
            device_id={"pipe": below},
            device_id_type=MESH,
        )

    def chain_arrival(p, c, slot):
        rows = pl.ds(pl.multiple_of(p * piece_rows, piece_rows), piece_rows)
        return pltpu.make_async_remote_copy(
            src_ref=back.at[c, rows],
            dst_ref=g_in.at[slot, c, rows],
            send_sem=chain_sems.at[0, p, c],
            recv_sem=chain_sems.at[1, p, c],
            device_id={"pipe": below},
            device_id_type=MESH,
        )

    def piece(p, carry):
        rows = pl.ds(pl.multiple_of(p * piece_rows, piece_rows), piece_rows)

        total = jnp.zeros((piece_rows, 1), F32)
        for c in range(CHUNKS):

            @pl.when(s < last)
            def _():
                chain_arrival(p, c, 0).wait_recv()

            part = slice(c * chunk, (c + 1) * chunk)
            grad = (g_in[0, c, rows].astype(F32) * scale_ref[:, part]).astype(BF16)
            bg[rows, part] = grad
            for f in range(tiles):
                cols = slice(f * F_TILE, (f + 1) * F_TILE)
                act_grad = jnp.dot(grad, down_t[part, cols], preferred_element_type=F32)
                if c > 0:
                    act_grad = act_grad + partial[:, cols]
                if c < CHUNKS - 1:
                    partial[:, cols] = act_grad
                else:
                    rounded = (act_grad * slope[rows, cols]).astype(BF16)
                    hg[rows, cols] = rounded
                    total += jnp.sum(
                        rounded.astype(F32) * hidden[rows, cols], axis=-1, keepdims=True
                    )
        mean = total * (1.0 / width)
        inv = inverse[rows, 0:1]
        hidden_grad = hg[rows, :]
        for c in range(CHUNKS):
            cols = slice(c * chunk, (c + 1) * chunk)
            normed_grad = jnp.dot(hidden_grad, up_t[:, cols], preferred_element_type=F32)
            unit_part = unit[rows, cols]
            back[c, rows] = (
                g_in[0, c, rows].astype(F32)
                + inv * (normed_grad * gain_ref[:, cols] - unit_part * mean)
            ).astype(BF16)
            chain_copy(p, c).start()
            gain_acc[:, cols] += jnp.sum(normed_grad * unit_part, axis=0, keepdims=True)
        return carry

    lax.fori_loop(0, PIECES, piece, 0)

    @pl.when(early)
    def _():
        lax.fori_loop(0, width // F_TILE, branch_tile, 0)

    stats[z, 0:1, :] = gain_acc[...]
    for c in range(CHUNKS):
        cols = slice(c * chunk, (c + 1) * chunk)
        stats[z, 1:2, cols] = jnp.sum(
            g_in[0, c].astype(F32) * branch[:, cols], axis=0, keepdims=True
        )

    rest = down_rows // 4
    main = down_rows - rest
    half = width // 2
    slots = (
        (rs_send_a, rs_recv_a, rest_in_a, rest_send_a, rest_recv_a, rest_own_a),
        (rs_send_b, rs_recv_b, rest_in_b, rest_send_b, rest_recv_b, rest_own_b),
    )

    def own_part(dest, first, size, cols):
        rows = pl.ds(pl.multiple_of(dest * down_rows + first, 32), size)
        return jnp.dot(act_t[rows, :], bg[:, cols], preferred_element_type=F32)

    def rs_copy(way, side, size, j):
        sent, received = slots[way][:2]
        return pltpu.make_async_remote_copy(
            src_ref=sent.at[side, j, pl.ds(0, size)],
            dst_ref=received.at[side, j, pl.ds(0, size)],
            send_sem=rs_sems.at[0, side, way, j],
            recv_sem=rs_sems.at[1, side, way, j],
            device_id=target_of(way),
            device_id_type=MESH,
        )

    def rest_copy(way, j):
        return pltpu.make_async_remote_copy(
            src_ref=slots[way][5].at[j],
            dst_ref=slots[way][2].at[j],
            send_sem=rest_sems.at[0, way, j],
            recv_sem=rest_sems.at[1, way, j],
            device_id={"pipe": other},
            device_id_type=MESH,
        )

    def rest_ring_copy(way, j):
        return pltpu.make_async_remote_copy(
            src_ref=slots[way][2].at[0] if j == 0 else slots[way][3].at[j],
            dst_ref=slots[way][4].at[j],
            send_sem=rest_ring_sems.at[0, way, j],
            recv_sem=rest_ring_sems.at[1, way, j],
            device_id=target_of(way),
            device_id_type=MESH,
        )

    def back_copy():
        return pltpu.make_async_remote_copy(
            src_ref=rest_out,
            dst_ref=rest_back,
            send_sem=back_sems.at[0],
            recv_sem=back_sems.at[1],
            device_id={"pipe": partner},
            device_id_type=MESH,
        )

    def stat_copy(way, j, arrival=False):
        ahead = j + 1 if arrival else j
        owner = lax.rem(z - ahead + ring, ring) if way == 0 else lax.rem(z + ahead, ring)
        return pltpu.make_async_remote_copy(
            src_ref=stats.at[owner],
            dst_ref=stats.at[owner],
            send_sem=stat_sems.at[0, way, j],
            recv_sem=stat_sems.at[1, way, j],
            device_id={"dp": right if way == 0 else left},
            device_id_type=MESH,
        )

    sides = (slice(0, half), slice(half, width))

    def rs_part(way, side, size, j, dest):
        sent, received = slots[way][:2]
        value = own_part(dest, 0, size, sides[side])

        @pl.when(j == 0)
        def _():
            sent[side, j, 0:size] = value.astype(BF16)

        @pl.when(j > 0)
        def _():
            rs_copy(way, side, size, j - 1).wait_recv()
            sent[side, j, 0:size] = (
                value + received[side, j - 1, 0:size].astype(F32)
            ).astype(BF16)

        rs_copy(way, side, size, j).start()

    def rest_part(way, j):
        hops = ways[way][1]

        @pl.when(j < hops)
        def _():
            dest = owner_at(1 - way, hops - j)
            for cols in sides:
                slots[way][5][j, :, cols] = own_part(dest, main, rest, cols).astype(BF16)
            rest_copy(way, j).start()

    def rs_step(j, size):
        for side in range(2):
            for way, hops in ways:

                @pl.when(j < hops)
                def _():
                    rs_part(way, side, size, j, owner_at(1 - way, hops - j))

        for way, hops in ways:

            @pl.when(j < hops)
            def _():
                @pl.when(j > 0)
                def _():
                    stat_copy(way, j - 1, True).wait_recv()

                stat_copy(way, j).start()

    def rs_step_late(j, carry):
        @pl.when(j < hops_a // 2)
        def _():
            for ahead in range(2):
                for way in range(2):
                    rest_part(way, 2 * j + ahead)

        rs_step(j, main)
        return carry

    def rs_step_full(j, carry):
        rs_step(j, down_rows)
        return carry

    def finish(size):
        for side in range(2):
            cols = sides[side]
            value = own_sum[0:size, cols]
            for way, hops in ways:
                rs_copy(way, side, size, hops - 1).wait_recv()
                value = value + slots[way][1][side, hops - 1, 0:size].astype(F32)
            out_ref[0, 0:size, cols] = value.astype(BF16)

    @pl.when(late)
    def _():
        lax.fori_loop(0, hops_a, rs_step_late, 0)
        for cols in sides:
            own_sum[:, cols] = own_part(z, 0, down_rows, cols)
        finish(main)
        back_copy().wait_recv()
        out_ref[0, main:] = (own_sum[main:] + rest_back[...].astype(F32)).astype(BF16)

    @pl.when(jnp.logical_not(late))
    def _():
        lax.fori_loop(0, hops_a, rs_step_full, 0)
        for cols in sides:
            own_sum[:, cols] = own_part(z, 0, down_rows, cols)
        finish(down_rows)


    @pl.when(early)
    def _():
        for j in range(hops_a):
            for way, hops in ways:
                if j < hops:
                    rest_copy(way, j).wait_recv()
                    if j > 0:
                        rest_ring_copy(way, j - 1).wait_recv()
                        slots[way][3][j] = (
                            slots[way][2][j].astype(F32) + slots[way][4][j - 1].astype(F32)
                        ).astype(BF16)
                    rest_ring_copy(way, j).start()
        total = jnp.zeros((rest, width), F32)
        for way, hops in ways:
            rest_ring_copy(way, hops - 1).wait_recv()
            total = total + slots[way][4][hops - 1].astype(F32)
        rest_out[...] = total.astype(BF16)
        back_copy().start()

    for way, hops in ways:
        stat_copy(way, hops - 1, True).wait_recv()
    summed = stats[0]
    for i in range(1, ring):
        summed = summed + stats[i]
    gain_out[...] = summed[0:1]
    scale_out[...] = summed[1:2]

    for way, hops in ways:
        for step in range(hops):
            for kind in range(2):
                gather_copy(kind, 0, way, step).wait_send()
            stat_copy(way, step).wait_send()

    @pl.when(jnp.logical_not(early))
    def _():
        for way, hops in ways:
            for step in range(hops):
                for kind in range(2):
                    gather_copy(kind, 1, way, step).wait_send()

    @pl.when(jnp.logical_not(late))
    def _():
        for way, hops in ways:
            for step in range(hops):
                for side in range(2):
                    rs_copy(way, side, down_rows, step).wait_send()

    @pl.when(early)
    def _():
        for kind in range(2):
            seed_copy(kind).wait_send()
        for way, hops in ways:
            for step in range(hops):
                rest_ring_copy(way, step).wait_send()
        back_copy().wait_send()

    @pl.when(late)
    def _():
        for way, hops in ways:
            for step in range(hops):
                for kind in range(2):
                    help_copy(kind, way, step).wait_send()
                    forward_copy(kind, way, step).wait_send()
                for side in range(2):
                    rs_copy(way, side, main, step).wait_send()
                rest_copy(way, step).wait_send()

    for p in range(PIECES):
        for c in range(CHUNKS):
            chain_copy(p, c).wait_send()

    @pl.when(s == last)
    def _():
        for p in range(PIECES):
            for c in range(CHUNKS):
                chain_arrival(p, c, 1).wait_recv()


def shards(stages, ring, x_saved, up_weights, down_weights, norm_gain, layer_scale, cotangent, lengths):
    unused, rows, width = x_saved.shape
    ff = up_weights.shape[2]
    down_rows = down_weights.shape[1]
    tokens = rows * 5 // 8
    hops_a = ring // 2
    hops_b = ring - 1 - hops_a
    vmem = pl.BlockSpec(memory_space=pltpu.VMEM)
    smem = pl.BlockSpec(memory_space=pltpu.SMEM)
    return pl.pallas_call(
        functools.partial(kernel, stages, ring),
        out_shape=(
            jax.ShapeDtypeStruct((1, down_rows, width), BF16),
            jax.ShapeDtypeStruct((1, width), F32),
            jax.ShapeDtypeStruct((1, width), F32),
        ),
        in_specs=[smem] + [vmem] * 6,
        out_specs=(vmem, vmem, vmem),
        scratch_shapes=[
            pltpu.VMEM((width, ff), BF16),
            pltpu.VMEM((ff, width), BF16),
            pltpu.VMEM((ff, width), BF16),
            pltpu.VMEM((width, ff), BF16),
            pltpu.VMEM((tokens, ff), F32),
            pltpu.VMEM((tokens, ff), F32),
            pltpu.VMEM((tokens, ff), BF16),
            pltpu.VMEM((ff, tokens), BF16),
            pltpu.VMEM((tokens, width), F32),
            pltpu.VMEM((tokens, 128), F32),
            pltpu.VMEM((tokens, width), BF16),
            pltpu.VMEM((tokens, width), F32),
            pltpu.VMEM((tokens, width), BF16),
            pltpu.VMEM((2, CHUNKS, tokens, width // CHUNKS), BF16),
            pltpu.VMEM((CHUNKS, tokens, width // CHUNKS), BF16),
            pltpu.VMEM((tokens, width), BF16),
            pltpu.VMEM((tokens, ff), BF16),
            pltpu.VMEM((1, width), F32),
            pltpu.VMEM((tokens // PIECES, ff), F32),
            pltpu.VMEM((ring, 2, width), F32),
            pltpu.VMEM((2, hops_a, down_rows, width // 2), BF16),
            pltpu.VMEM((2, hops_a, down_rows, width // 2), BF16),
            pltpu.VMEM((2, hops_b, down_rows, width // 2), BF16),
            pltpu.VMEM((2, hops_b, down_rows, width // 2), BF16),
            pltpu.VMEM((hops_a, down_rows // 4, width), BF16),
            pltpu.VMEM((hops_b, down_rows // 4, width), BF16),
            pltpu.VMEM((down_rows, width), F32),
            pltpu.VMEM((width // 4, ff), BF16),
            pltpu.VMEM((ff * 3 // 8, width), BF16),
            pltpu.VMEM((hops_a, down_rows // 4, width), BF16),
            pltpu.VMEM((hops_b, down_rows // 4, width), BF16),
            pltpu.VMEM((hops_a, down_rows // 4, width), BF16),
            pltpu.VMEM((hops_b, down_rows // 4, width), BF16),
            pltpu.VMEM((hops_a, down_rows // 4, width), BF16),
            pltpu.VMEM((hops_b, down_rows // 4, width), BF16),
            pltpu.VMEM((down_rows // 4, width), BF16),
            pltpu.VMEM((down_rows // 4, width), BF16),
            pltpu.SemaphoreType.DMA((2, 2, 2, 2, hops_a)),
            pltpu.SemaphoreType.DMA((3, 2, 2, hops_a)),
            pltpu.SemaphoreType.DMA((2, 2)),
            pltpu.SemaphoreType.DMA((2, PIECES, CHUNKS)),
            pltpu.SemaphoreType.DMA((2, 2, 2, hops_a)),
            pltpu.SemaphoreType.DMA((2, 2, hops_a)),
            pltpu.SemaphoreType.DMA((2, 2, hops_a)),
            pltpu.SemaphoreType.DMA((2,)),
            pltpu.SemaphoreType.DMA((2, 2, hops_a)),
        ],
        compiler_params=pltpu.CompilerParams(
            collective_id=0,
            has_side_effects=True,
            vmem_limit_bytes=60 * 1024 * 1024,
        ),
        name="layer_chain",
    )(lengths, up_weights, down_weights, x_saved, cotangent, norm_gain, layer_scale)


def solution(mesh):
    return jax.shard_map(
        functools.partial(shards, mesh.shape["pipe"], mesh.shape["dp"]),
        mesh=mesh,
        in_specs=(
            P("pipe", "dp", None),
            P("pipe", "dp", None),
            P("pipe", "dp", None),
            P("pipe", None),
            P("pipe", None),
            P("dp", None),
            P("dp", None),
        ),
        out_specs=(P("pipe", "dp", None), P("pipe", None), P("pipe", None)),
        check_vma=False,
    )
```

```python
import functools

import jax
import jax.numpy as jnp
from jax import lax
from jax.experimental import pallas as pl
from jax.experimental.pallas import tpu as pltpu
from jax.sharding import PartitionSpec as P

EPSILON = 1e-06
ROOT = 0.7978845608028654
CUBIC = 0.044715
PIECES = 5
CHUNKS = 2
F_TILE = 512
LAG = 2
HELP_LAG = 1
MESH = pl.DeviceIdType.MESH
F32 = jnp.float32
BF16 = jnp.bfloat16


def kernel(
    stages,
    ring,
    len_ref,
    up_ref,
    down_ref,
    x_ref,
    cot_ref,
    gain_ref,
    scale_ref,
    out_ref,
    gain_out,
    scale_out,
    up_w,
    down_w,
    up_t,
    down_t,
    hidden,
    slope,
    act,
    act_t,
    unit,
    inverse,
    normed,
    branch,
    start,
    g_in,
    back,
    bg,
    hg,
    gain_acc,
    partial,
    stats,
    rs_send_a,
    rs_recv_a,
    rs_send_b,
    rs_recv_b,
    rest_own_a,
    rest_own_b,
    own_sum,
    help_up,
    help_down,
    rest_in_a,
    rest_in_b,
    rest_send_a,
    rest_send_b,
    rest_recv_a,
    rest_recv_b,
    rest_out,
    rest_back,
    ag_sems,
    help_sems,
    seed_sems,
    chain_sems,
    rs_sems,
    rest_sems,
    rest_ring_sems,
    back_sems,
    stat_sems,
):
    s = lax.axis_index("pipe")
    z = lax.axis_index("dp")
    last = stages - 1
    right = lax.rem(z + 1, ring)
    left = lax.rem(z + ring - 1, ring)
    above = lax.rem(s + 1, stages)
    below = lax.rem(s + stages - 1, stages)
    width, ff = up_w.shape
    up_rows = up_ref.shape[1]
    down_rows = down_ref.shape[1]
    tokens = normed.shape[0]
    slot = x_ref.shape[1] // 2
    hops_a = ring // 2
    hops_b = ring - 1 - hops_a
    piece_rows = tokens // PIECES
    chunk = width // CHUNKS

    barrier = pltpu.get_barrier_semaphore()
    quarter = stages // 4
    partner = lax.rem(s + quarter, stages)
    other = lax.rem(s + stages - quarter, stages)
    for place in (
        {"dp": right},
        {"dp": left},
        {"pipe": above},
        {"pipe": below},
        {"pipe": partner},
        {"pipe": other},
    ):
        pl.semaphore_signal(barrier, inc=1, device_id=place, device_id_type=MESH)
    pl.semaphore_wait(barrier, 6)
    early = s >= stages - quarter
    late = s < quarter

    up_rest = up_rows // 4
    down_rest = down_rows * 3 // 8
    ways = ((0, hops_a), (1, hops_b))
    weights = (
        (up_w, up_rows, up_rest, up_ref, help_up),
        (down_w, down_rows, down_rest, down_ref, help_down),
    )

    def owner_at(way, distance):
        if way == 0:
            return lax.rem(z - distance + ring, ring)
        return lax.rem(z + distance, ring)

    def target_of(way):
        return {"dp": right if way == 0 else left}

    def block_of(kind, part, owner):
        buffer, rows, rest, own, helper = weights[kind]
        first, size = (0, rows - rest) if part == 0 else (rows - rest, rest)
        return buffer.at[pl.ds(pl.multiple_of(owner * rows + first, 16), size)]

    def own_block(kind, part):
        buffer, rows, rest, own, helper = weights[kind]
        first, size = (0, rows - rest) if part == 0 else (rows - rest, rest)
        return own.at[0, pl.ds(first, size)]

    def gather_copy(kind, part, way, step, arrival=False):
        block = block_of(kind, part, owner_at(way, step + 1 if arrival else step))
        return pltpu.make_async_remote_copy(
            src_ref=own_block(kind, part) if step == 0 and not arrival else block,
            dst_ref=block,
            send_sem=ag_sems.at[0, kind, part, way, step],
            recv_sem=ag_sems.at[1, kind, part, way, step],
            device_id=target_of(way),
            device_id_type=MESH,
        )

    def gather_part(kind, part, step):
        for way, hops in ways:
            if step > 0 and step <= hops:
                gather_copy(kind, part, way, step - 1, True).wait_recv()
            if step < hops:
                gather_copy(kind, part, way, step).start()

    def gather_step(kind, step):
        gather_part(kind, 0, step)

        @pl.when(jnp.logical_not(early))
        def _():
            gather_part(kind, 1, step)

    def rest_arrivals(kind, steps):
        @pl.when(early)
        def _():
            for step in steps:
                for way, hops in ways:
                    if step > 0 and step <= hops:
                        gather_copy(kind, 1, way, step - 1, True).wait_recv()

    def help_block(kind, owner):
        buffer, rows, rest, own, helper = weights[kind]
        return helper.at[pl.ds(pl.multiple_of(owner * rest, 16), rest)]

    def seed_copy(kind):
        return pltpu.make_async_remote_copy(
            src_ref=own_block(kind, 1),
            dst_ref=help_block(kind, z),
            send_sem=seed_sems.at[0, kind],
            recv_sem=seed_sems.at[1, kind],
            device_id={"pipe": partner},
            device_id_type=MESH,
        )

    def help_copy(kind, way, step, arrival=False):
        block = help_block(kind, owner_at(way, step + 1 if arrival else step))
        return pltpu.make_async_remote_copy(
            src_ref=block,
            dst_ref=block,
            send_sem=help_sems.at[0, kind, way, step],
            recv_sem=help_sems.at[1, kind, way, step],
            device_id=target_of(way),
            device_id_type=MESH,
        )

    def forward_copy(kind, way, step):
        owner = owner_at(way, step + 1)
        return pltpu.make_async_remote_copy(
            src_ref=help_block(kind, owner),
            dst_ref=block_of(kind, 1, owner),
            send_sem=help_sems.at[2, kind, way, step],
            recv_sem=ag_sems.at[1, kind, 1, way, step],
            device_id={"pipe": other},
            device_id_type=MESH,
        )

    @pl.when(early)
    def _():
        for kind in range(2):
            seed_copy(kind).start()

    @pl.when(late)
    def _():
        for kind in range(2):
            seed_copy(kind).wait_recv()
        for turn in range(hops_a + 1 + HELP_LAG):
            for kind, step in ((0, turn), (1, turn - HELP_LAG)):
                for way, hops in ways:
                    if step > 0 and step <= hops:
                        help_copy(kind, way, step - 1, True).wait_recv()
                    if step >= 0 and step < hops:
                        help_copy(kind, way, step).start()
                    if step > 0 and step <= hops:
                        forward_copy(kind, way, step - 1).start()

    gather_step(0, 0)
    for buffer, rows, rest, own, helper in weights:
        buffer[pl.ds(pl.multiple_of(z * rows, rows), rows)] = own[0]

    first_len = len_ref[0, 0]
    row = lax.broadcasted_iota(jnp.int32, (tokens, x_ref.shape[1]), 0)
    col = lax.broadcasted_iota(jnp.int32, (tokens, x_ref.shape[1]), 1)
    source = jnp.where(row < first_len, row, row + (slot - first_len))
    pick = (col == source).astype(F32).astype(BF16)
    x_rows = jnp.dot(pick, x_ref[0], preferred_element_type=F32)
    scaled = lax.rsqrt(jnp.mean(x_rows * x_rows, axis=-1, keepdims=True) + EPSILON)
    inverse[...] = jnp.broadcast_to(scaled, inverse.shape)
    unit_rows = x_rows * scaled
    unit[...] = unit_rows
    normed[...] = (unit_rows * gain_ref[...]).astype(BF16)
    start[...] = jnp.dot(pick, cot_ref[...], preferred_element_type=F32).astype(BF16)
    gain_acc[...] = jnp.zeros_like(gain_acc)

    def hidden_tile(tile):
        cols = pl.ds(pl.multiple_of(tile * F_TILE, F_TILE), F_TILE)
        h = jnp.dot(normed[...], up_w[:, cols], preferred_element_type=F32)
        square = h * h
        th = jnp.tanh(ROOT * (h + CUBIC * (square * h)))
        half = 0.5 * (1.0 + th)
        a = h * half
        hidden[:, cols] = h
        slope[:, cols] = half + 0.5 * h * (1.0 - th * th) * (
            ROOT * (1.0 + (3.0 * CUBIC) * square)
        )
        act[:, cols] = a.astype(BF16)
        act_t[cols, :] = a.T.astype(BF16)

    def turn_up(block, carry):
        rows = pl.ds(pl.multiple_of(block * 128, 128), 128)
        up_t[:, rows] = up_w[rows, :].T
        return carry

    def turn_down(owner):
        for part in range(down_rows // 128):
            rows = pl.ds(pl.multiple_of(owner * down_rows + part * 128, 128), 128)
            down_t[:, rows] = down_w[rows, :].T

    turn_down(z)
    blocks = width // 128
    tiles = ff // F_TILE
    for step in range(1, hops_a + LAG + 1):
        if step <= hops_a:
            gather_step(0, step)
        if step == hops_a:
            rest_arrivals(0, range(1, hops_a + 1))
        if step >= LAG:
            gather_step(1, step - LAG)
            done = step - LAG
            rest_arrivals(1, (done,))
            if done > 0 and done <= hops_a:
                turn_down(lax.rem(z - done + ring, ring))
            if done > 0 and done <= hops_b:
                turn_down(lax.rem(z + done, ring))
        if step >= hops_a and step < hops_a + LAG:
            part = step - hops_a
            lax.fori_loop(
                part * tiles // LAG,
                (part + 1) * tiles // LAG,
                lambda tile, c: (hidden_tile(tile), c)[1],
                0,
            )
            lax.fori_loop(part * blocks // LAG, (part + 1) * blocks // LAG, turn_up, 0)

    @pl.when(s == last)
    def _():
        for c in range(CHUNKS):
            g_in[0, c] = start[:, c * chunk : (c + 1) * chunk]

    def branch_tile(tile, carry):
        cols = pl.ds(pl.multiple_of(tile * F_TILE, F_TILE), F_TILE)
        branch[:, cols] = jnp.dot(act[...], down_w[:, cols], preferred_element_type=F32)
        return carry

    @pl.when(s < 2)
    def _():
        lax.fori_loop(0, width // F_TILE, branch_tile, 0)

    landing = jnp.where(s == 0, 1, 0)

    def chain_copy(p, c):
        rows = pl.ds(pl.multiple_of(p * piece_rows, piece_rows), piece_rows)
        return pltpu.make_async_remote_copy(
            src_ref=back.at[c, rows],
            dst_ref=g_in.at[landing, c, rows],
            send_sem=chain_sems.at[0, p, c],
            recv_sem=chain_sems.at[1, p, c],
            device_id={"pipe": below},
            device_id_type=MESH,
        )

    def chain_arrival(p, c, slot):
        rows = pl.ds(pl.multiple_of(p * piece_rows, piece_rows), piece_rows)
        return pltpu.make_async_remote_copy(
            src_ref=back.at[c, rows],
            dst_ref=g_in.at[slot, c, rows],
            send_sem=chain_sems.at[0, p, c],
            recv_sem=chain_sems.at[1, p, c],
            device_id={"pipe": below},
            device_id_type=MESH,
        )

    def piece(p, carry):
        rows = pl.ds(pl.multiple_of(p * piece_rows, piece_rows), piece_rows)

        total = jnp.zeros((piece_rows, 1), F32)
        for c in range(CHUNKS):

            @pl.when(s < last)
            def _():
                chain_arrival(p, c, 0).wait_recv()

            part = slice(c * chunk, (c + 1) * chunk)
            grad = (g_in[0, c, rows].astype(F32) * scale_ref[:, part]).astype(BF16)
            bg[rows, part] = grad
            for f in range(ff // F_TILE):
                cols = slice(f * F_TILE, (f + 1) * F_TILE)
                act_grad = jnp.dot(grad, down_t[part, cols], preferred_element_type=F32)
                if c > 0:
                    act_grad = act_grad + partial[:, cols]
                if c < CHUNKS - 1:
                    partial[:, cols] = act_grad
                else:
                    rounded = (act_grad * slope[rows, cols]).astype(BF16)
                    hg[rows, cols] = rounded
                    total += jnp.sum(
                        rounded.astype(F32) * hidden[rows, cols], axis=-1, keepdims=True
                    )
        mean = total * (1.0 / width)
        inv = inverse[rows, 0:1]
        hidden_grad = hg[rows, :]
        for c in range(CHUNKS):
            cols = slice(c * chunk, (c + 1) * chunk)
            normed_grad = jnp.dot(hidden_grad, up_t[:, cols], preferred_element_type=F32)
            unit_part = unit[rows, cols]
            back[c, rows] = (
                g_in[0, c, rows].astype(F32)
                + inv * (normed_grad * gain_ref[:, cols] - unit_part * mean)
            ).astype(BF16)
            chain_copy(p, c).start()
            gain_acc[:, cols] += jnp.sum(normed_grad * unit_part, axis=0, keepdims=True)
        return carry

    lax.fori_loop(0, PIECES, piece, 0)

    @pl.when(s >= 2)
    def _():
        lax.fori_loop(0, width // F_TILE, branch_tile, 0)

    stats[z, 0:1, :] = gain_acc[...]
    for c in range(CHUNKS):
        cols = slice(c * chunk, (c + 1) * chunk)
        stats[z, 1:2, cols] = jnp.sum(
            g_in[0, c].astype(F32) * branch[:, cols], axis=0, keepdims=True
        )

    rest = down_rows // 4
    main = down_rows - rest
    half = width // 2
    slots = (
        (rs_send_a, rs_recv_a, rest_in_a, rest_send_a, rest_recv_a, rest_own_a),
        (rs_send_b, rs_recv_b, rest_in_b, rest_send_b, rest_recv_b, rest_own_b),
    )

    def own_part(dest, first, size, cols):
        rows = pl.ds(pl.multiple_of(dest * down_rows + first, 32), size)
        return jnp.dot(act_t[rows, :], bg[:, cols], preferred_element_type=F32)

    def rs_copy(way, side, size, j):
        sent, received = slots[way][:2]
        return pltpu.make_async_remote_copy(
            src_ref=sent.at[side, j, pl.ds(0, size)],
            dst_ref=received.at[side, j, pl.ds(0, size)],
            send_sem=rs_sems.at[0, side, way, j],
            recv_sem=rs_sems.at[1, side, way, j],
            device_id=target_of(way),
            device_id_type=MESH,
        )

    def rest_copy(way, j):
        return pltpu.make_async_remote_copy(
            src_ref=slots[way][5].at[j],
            dst_ref=slots[way][2].at[j],
            send_sem=rest_sems.at[0, way, j],
            recv_sem=rest_sems.at[1, way, j],
            device_id={"pipe": other},
            device_id_type=MESH,
        )

    def rest_ring_copy(way, j):
        return pltpu.make_async_remote_copy(
            src_ref=slots[way][2].at[0] if j == 0 else slots[way][3].at[j],
            dst_ref=slots[way][4].at[j],
            send_sem=rest_ring_sems.at[0, way, j],
            recv_sem=rest_ring_sems.at[1, way, j],
            device_id=target_of(way),
            device_id_type=MESH,
        )

    def back_copy():
        return pltpu.make_async_remote_copy(
            src_ref=rest_out,
            dst_ref=rest_back,
            send_sem=back_sems.at[0],
            recv_sem=back_sems.at[1],
            device_id={"pipe": partner},
            device_id_type=MESH,
        )

    def stat_copy(way, j, arrival=False):
        ahead = j + 1 if arrival else j
        owner = lax.rem(z - ahead + ring, ring) if way == 0 else lax.rem(z + ahead, ring)
        return pltpu.make_async_remote_copy(
            src_ref=stats.at[owner],
            dst_ref=stats.at[owner],
            send_sem=stat_sems.at[0, way, j],
            recv_sem=stat_sems.at[1, way, j],
            device_id={"dp": right if way == 0 else left},
            device_id_type=MESH,
        )

    sides = (slice(0, half), slice(half, width))

    def rs_part(way, side, size, j, dest):
        sent, received = slots[way][:2]
        value = own_part(dest, 0, size, sides[side])

        @pl.when(j == 0)
        def _():
            sent[side, j, 0:size] = value.astype(BF16)

        @pl.when(j > 0)
        def _():
            rs_copy(way, side, size, j - 1).wait_recv()
            sent[side, j, 0:size] = (
                value + received[side, j - 1, 0:size].astype(F32)
            ).astype(BF16)

        rs_copy(way, side, size, j).start()

    def rest_part(way, j):
        hops = ways[way][1]

        @pl.when(j < hops)
        def _():
            dest = owner_at(1 - way, hops - j)
            for cols in sides:
                slots[way][5][j, :, cols] = own_part(dest, main, rest, cols).astype(BF16)
            rest_copy(way, j).start()

    def rs_step(j, size):
        for side in range(2):
            for way, hops in ways:

                @pl.when(j < hops)
                def _():
                    rs_part(way, side, size, j, owner_at(1 - way, hops - j))

        for way, hops in ways:

            @pl.when(j < hops)
            def _():
                @pl.when(j > 0)
                def _():
                    stat_copy(way, j - 1, True).wait_recv()

                stat_copy(way, j).start()

    def rs_step_late(j, carry):
        @pl.when(j < hops_a // 2)
        def _():
            for ahead in range(2):
                for way in range(2):
                    rest_part(way, 2 * j + ahead)

        rs_step(j, main)
        return carry

    def rs_step_full(j, carry):
        rs_step(j, down_rows)
        return carry

    def finish(size):
        for side in range(2):
            cols = sides[side]
            value = own_sum[0:size, cols]
            for way, hops in ways:
                rs_copy(way, side, size, hops - 1).wait_recv()
                value = value + slots[way][1][side, hops - 1, 0:size].astype(F32)
            out_ref[0, 0:size, cols] = value.astype(BF16)

    @pl.when(late)
    def _():
        lax.fori_loop(0, hops_a, rs_step_late, 0)
        for cols in sides:
            own_sum[:, cols] = own_part(z, 0, down_rows, cols)
        finish(main)
        back_copy().wait_recv()
        out_ref[0, main:] = (own_sum[main:] + rest_back[...].astype(F32)).astype(BF16)

    @pl.when(jnp.logical_not(late))
    def _():
        lax.fori_loop(0, hops_a, rs_step_full, 0)
        for cols in sides:
            own_sum[:, cols] = own_part(z, 0, down_rows, cols)
        finish(down_rows)


    @pl.when(early)
    def _():
        for j in range(hops_a):
            for way, hops in ways:
                if j < hops:
                    rest_copy(way, j).wait_recv()
                    if j > 0:
                        rest_ring_copy(way, j - 1).wait_recv()
                        slots[way][3][j] = (
                            slots[way][2][j].astype(F32) + slots[way][4][j - 1].astype(F32)
                        ).astype(BF16)
                    rest_ring_copy(way, j).start()
        total = jnp.zeros((rest, width), F32)
        for way, hops in ways:
            rest_ring_copy(way, hops - 1).wait_recv()
            total = total + slots[way][4][hops - 1].astype(F32)
        rest_out[...] = total.astype(BF16)
        back_copy().start()

    for way, hops in ways:
        stat_copy(way, hops - 1, True).wait_recv()
    summed = stats[0]
    for i in range(1, ring):
        summed = summed + stats[i]
    gain_out[...] = summed[0:1]
    scale_out[...] = summed[1:2]

    for way, hops in ways:
        for step in range(hops):
            for kind in range(2):
                gather_copy(kind, 0, way, step).wait_send()
            stat_copy(way, step).wait_send()

    @pl.when(jnp.logical_not(early))
    def _():
        for way, hops in ways:
            for step in range(hops):
                for kind in range(2):
                    gather_copy(kind, 1, way, step).wait_send()

    @pl.when(jnp.logical_not(late))
    def _():
        for way, hops in ways:
            for step in range(hops):
                for side in range(2):
                    rs_copy(way, side, down_rows, step).wait_send()

    @pl.when(early)
    def _():
        for kind in range(2):
            seed_copy(kind).wait_send()
        for way, hops in ways:
            for step in range(hops):
                rest_ring_copy(way, step).wait_send()
        back_copy().wait_send()

    @pl.when(late)
    def _():
        for way, hops in ways:
            for step in range(hops):
                for kind in range(2):
                    help_copy(kind, way, step).wait_send()
                    forward_copy(kind, way, step).wait_send()
                for side in range(2):
                    rs_copy(way, side, main, step).wait_send()
                rest_copy(way, step).wait_send()

    for p in range(PIECES):
        for c in range(CHUNKS):
            chain_copy(p, c).wait_send()

    @pl.when(s == last)
    def _():
        for p in range(PIECES):
            for c in range(CHUNKS):
                chain_arrival(p, c, 1).wait_recv()


def shards(stages, ring, x_saved, up_weights, down_weights, norm_gain, layer_scale, cotangent, lengths):
    unused, rows, width = x_saved.shape
    ff = up_weights.shape[2]
    down_rows = down_weights.shape[1]
    tokens = rows * 5 // 8
    hops_a = ring // 2
    hops_b = ring - 1 - hops_a
    vmem = pl.BlockSpec(memory_space=pltpu.VMEM)
    smem = pl.BlockSpec(memory_space=pltpu.SMEM)
    return pl.pallas_call(
        functools.partial(kernel, stages, ring),
        out_shape=(
            jax.ShapeDtypeStruct((1, down_rows, width), BF16),
            jax.ShapeDtypeStruct((1, width), F32),
            jax.ShapeDtypeStruct((1, width), F32),
        ),
        in_specs=[smem] + [vmem] * 6,
        out_specs=(vmem, vmem, vmem),
        scratch_shapes=[
            pltpu.VMEM((width, ff), BF16),
            pltpu.VMEM((ff, width), BF16),
            pltpu.VMEM((ff, width), BF16),
            pltpu.VMEM((width, ff), BF16),
            pltpu.VMEM((tokens, ff), F32),
            pltpu.VMEM((tokens, ff), F32),
            pltpu.VMEM((tokens, ff), BF16),
            pltpu.VMEM((ff, tokens), BF16),
            pltpu.VMEM((tokens, width), F32),
            pltpu.VMEM((tokens, 128), F32),
            pltpu.VMEM((tokens, width), BF16),
            pltpu.VMEM((tokens, width), F32),
            pltpu.VMEM((tokens, width), BF16),
            pltpu.VMEM((2, CHUNKS, tokens, width // CHUNKS), BF16),
            pltpu.VMEM((CHUNKS, tokens, width // CHUNKS), BF16),
            pltpu.VMEM((tokens, width), BF16),
            pltpu.VMEM((tokens, ff), BF16),
            pltpu.VMEM((1, width), F32),
            pltpu.VMEM((tokens // PIECES, ff), F32),
            pltpu.VMEM((ring, 2, width), F32),
            pltpu.VMEM((2, hops_a, down_rows, width // 2), BF16),
            pltpu.VMEM((2, hops_a, down_rows, width // 2), BF16),
            pltpu.VMEM((2, hops_b, down_rows, width // 2), BF16),
            pltpu.VMEM((2, hops_b, down_rows, width // 2), BF16),
            pltpu.VMEM((hops_a, down_rows // 4, width), BF16),
            pltpu.VMEM((hops_b, down_rows // 4, width), BF16),
            pltpu.VMEM((down_rows, width), F32),
            pltpu.VMEM((width // 4, ff), BF16),
            pltpu.VMEM((ff * 3 // 8, width), BF16),
            pltpu.VMEM((hops_a, down_rows // 4, width), BF16),
            pltpu.VMEM((hops_b, down_rows // 4, width), BF16),
            pltpu.VMEM((hops_a, down_rows // 4, width), BF16),
            pltpu.VMEM((hops_b, down_rows // 4, width), BF16),
            pltpu.VMEM((hops_a, down_rows // 4, width), BF16),
            pltpu.VMEM((hops_b, down_rows // 4, width), BF16),
            pltpu.VMEM((down_rows // 4, width), BF16),
            pltpu.VMEM((down_rows // 4, width), BF16),
            pltpu.SemaphoreType.DMA((2, 2, 2, 2, hops_a)),
            pltpu.SemaphoreType.DMA((3, 2, 2, hops_a)),
            pltpu.SemaphoreType.DMA((2, 2)),
            pltpu.SemaphoreType.DMA((2, PIECES, CHUNKS)),
            pltpu.SemaphoreType.DMA((2, 2, 2, hops_a)),
            pltpu.SemaphoreType.DMA((2, 2, hops_a)),
            pltpu.SemaphoreType.DMA((2, 2, hops_a)),
            pltpu.SemaphoreType.DMA((2,)),
            pltpu.SemaphoreType.DMA((2, 2, hops_a)),
        ],
        compiler_params=pltpu.CompilerParams(
            collective_id=0,
            has_side_effects=True,
            vmem_limit_bytes=60 * 1024 * 1024,
        ),
        name="layer_chain",
    )(lengths, up_weights, down_weights, x_saved, cotangent, norm_gain, layer_scale)


def solution(mesh):
    return jax.shard_map(
        functools.partial(shards, mesh.shape["pipe"], mesh.shape["dp"]),
        mesh=mesh,
        in_specs=(
            P("pipe", "dp", None),
            P("pipe", "dp", None),
            P("pipe", "dp", None),
            P("pipe", None),
            P("pipe", None),
            P("dp", None),
            P("dp", None),
        ),
        out_specs=(P("pipe", "dp", None), P("pipe", None), P("pipe", None)),
        check_vma=False,
    )
```

```python
import functools

import jax
import jax.numpy as jnp
from jax import lax
from jax.experimental import pallas as pl
from jax.experimental.pallas import tpu as pltpu
from jax.sharding import PartitionSpec as P

EPSILON = 1e-06
ROOT = 0.7978845608028654
CUBIC = 0.044715
PIECES = 5
CHUNKS = 2
F_TILE = 512
LAG = 2
HELP_LAG = 1
DEFER = 1
MESH = pl.DeviceIdType.MESH
F32 = jnp.float32
BF16 = jnp.bfloat16


def kernel(
    stages,
    ring,
    len_ref,
    up_ref,
    down_ref,
    x_ref,
    cot_ref,
    gain_ref,
    scale_ref,
    out_ref,
    gain_out,
    scale_out,
    up_w,
    down_w,
    up_t,
    down_t,
    hidden,
    slope,
    act,
    act_t,
    unit,
    inverse,
    normed,
    branch,
    start,
    g_in,
    back,
    bg,
    hg,
    gain_acc,
    partial,
    stats,
    rs_send_a,
    rs_recv_a,
    rs_send_b,
    rs_recv_b,
    rest_own_a,
    rest_own_b,
    own_sum,
    help_up,
    help_down,
    rest_in_a,
    rest_in_b,
    rest_send_a,
    rest_send_b,
    rest_recv_a,
    rest_recv_b,
    rest_out,
    rest_back,
    ag_sems,
    help_sems,
    seed_sems,
    chain_sems,
    rs_sems,
    rest_sems,
    rest_ring_sems,
    back_sems,
    stat_sems,
):
    s = lax.axis_index("pipe")
    z = lax.axis_index("dp")
    last = stages - 1
    right = lax.rem(z + 1, ring)
    left = lax.rem(z + ring - 1, ring)
    above = lax.rem(s + 1, stages)
    below = lax.rem(s + stages - 1, stages)
    width, ff = up_w.shape
    up_rows = up_ref.shape[1]
    down_rows = down_ref.shape[1]
    tokens = normed.shape[0]
    slot = x_ref.shape[1] // 2
    hops_a = ring // 2
    hops_b = ring - 1 - hops_a
    piece_rows = tokens // PIECES
    chunk = width // CHUNKS

    barrier = pltpu.get_barrier_semaphore()
    quarter = stages // 4
    partner = lax.rem(s + quarter, stages)
    other = lax.rem(s + stages - quarter, stages)
    for place in (
        {"dp": right},
        {"dp": left},
        {"pipe": above},
        {"pipe": below},
        {"pipe": partner},
        {"pipe": other},
    ):
        pl.semaphore_signal(barrier, inc=1, device_id=place, device_id_type=MESH)
    pl.semaphore_wait(barrier, 6)
    early = s >= stages - quarter
    late = s < quarter

    up_rest = up_rows // 4
    down_rest = down_rows * 3 // 8
    ways = ((0, hops_a), (1, hops_b))
    weights = (
        (up_w, up_rows, up_rest, up_ref, help_up),
        (down_w, down_rows, down_rest, down_ref, help_down),
    )

    def owner_at(way, distance):
        if way == 0:
            return lax.rem(z - distance + ring, ring)
        return lax.rem(z + distance, ring)

    def target_of(way):
        return {"dp": right if way == 0 else left}

    def block_of(kind, part, owner):
        buffer, rows, rest, own, helper = weights[kind]
        first, size = (0, rows - rest) if part == 0 else (rows - rest, rest)
        return buffer.at[pl.ds(pl.multiple_of(owner * rows + first, 16), size)]

    def own_block(kind, part):
        buffer, rows, rest, own, helper = weights[kind]
        first, size = (0, rows - rest) if part == 0 else (rows - rest, rest)
        return own.at[0, pl.ds(first, size)]

    def gather_copy(kind, part, way, step, arrival=False):
        block = block_of(kind, part, owner_at(way, step + 1 if arrival else step))
        return pltpu.make_async_remote_copy(
            src_ref=own_block(kind, part) if step == 0 and not arrival else block,
            dst_ref=block,
            send_sem=ag_sems.at[0, kind, part, way, step],
            recv_sem=ag_sems.at[1, kind, part, way, step],
            device_id=target_of(way),
            device_id_type=MESH,
        )

    def gather_part(kind, part, step):
        for way, hops in ways:
            if step > 0 and step <= hops:
                gather_copy(kind, part, way, step - 1, True).wait_recv()
            if step < hops:
                gather_copy(kind, part, way, step).start()

    def gather_step(kind, step):
        gather_part(kind, 0, step)

        @pl.when(jnp.logical_not(early))
        def _():
            gather_part(kind, 1, step)

    def rest_arrivals(kind, steps):
        @pl.when(early)
        def _():
            for step in steps:
                for way, hops in ways:
                    if step > 0 and step <= hops:
                        gather_copy(kind, 1, way, step - 1, True).wait_recv()

    def help_block(kind, owner):
        buffer, rows, rest, own, helper = weights[kind]
        return helper.at[pl.ds(pl.multiple_of(owner * rest, 16), rest)]

    def seed_copy(kind):
        return pltpu.make_async_remote_copy(
            src_ref=own_block(kind, 1),
            dst_ref=help_block(kind, z),
            send_sem=seed_sems.at[0, kind],
            recv_sem=seed_sems.at[1, kind],
            device_id={"pipe": partner},
            device_id_type=MESH,
        )

    def help_copy(kind, way, step, arrival=False):
        block = help_block(kind, owner_at(way, step + 1 if arrival else step))
        return pltpu.make_async_remote_copy(
            src_ref=block,
            dst_ref=block,
            send_sem=help_sems.at[0, kind, way, step],
            recv_sem=help_sems.at[1, kind, way, step],
            device_id=target_of(way),
            device_id_type=MESH,
        )

    def forward_copy(kind, way, step):
        owner = owner_at(way, step + 1)
        return pltpu.make_async_remote_copy(
            src_ref=help_block(kind, owner),
            dst_ref=block_of(kind, 1, owner),
            send_sem=help_sems.at[2, kind, way, step],
            recv_sem=ag_sems.at[1, kind, 1, way, step],
            device_id={"pipe": other},
            device_id_type=MESH,
        )

    @pl.when(early)
    def _():
        for kind in range(2):
            seed_copy(kind).start()

    @pl.when(late)
    def _():
        for kind in range(2):
            seed_copy(kind).wait_recv()
        for turn in range(hops_a + 1 + HELP_LAG):
            for kind, step in ((0, turn), (1, turn - HELP_LAG)):
                for way, hops in ways:
                    if step > 0 and step <= hops:
                        help_copy(kind, way, step - 1, True).wait_recv()
                    if step >= 0 and step < hops:
                        help_copy(kind, way, step).start()
                    if step > 0 and step <= hops:
                        forward_copy(kind, way, step - 1).start()

    gather_step(0, 0)
    for buffer, rows, rest, own, helper in weights:
        buffer[pl.ds(pl.multiple_of(z * rows, rows), rows)] = own[0]

    first_len = len_ref[0, 0]
    row = lax.broadcasted_iota(jnp.int32, (tokens, x_ref.shape[1]), 0)
    col = lax.broadcasted_iota(jnp.int32, (tokens, x_ref.shape[1]), 1)
    source = jnp.where(row < first_len, row, row + (slot - first_len))
    pick = (col == source).astype(F32).astype(BF16)
    x_rows = jnp.dot(pick, x_ref[0], preferred_element_type=F32)
    scaled = lax.rsqrt(jnp.mean(x_rows * x_rows, axis=-1, keepdims=True) + EPSILON)
    inverse[...] = jnp.broadcast_to(scaled, inverse.shape)
    unit_rows = x_rows * scaled
    unit[...] = unit_rows
    normed[...] = (unit_rows * gain_ref[...]).astype(BF16)
    start[...] = jnp.dot(pick, cot_ref[...], preferred_element_type=F32).astype(BF16)
    gain_acc[...] = jnp.zeros_like(gain_acc)

    def hidden_tile(tile):
        cols = pl.ds(pl.multiple_of(tile * F_TILE, F_TILE), F_TILE)
        h = jnp.dot(normed[...], up_w[:, cols], preferred_element_type=F32)
        square = h * h
        th = jnp.tanh(ROOT * (h + CUBIC * (square * h)))
        half = 0.5 * (1.0 + th)
        a = h * half
        hidden[:, cols] = h
        slope[:, cols] = half + 0.5 * h * (1.0 - th * th) * (
            ROOT * (1.0 + (3.0 * CUBIC) * square)
        )
        act[:, cols] = a.astype(BF16)
        act_t[cols, :] = a.T.astype(BF16)

    def turn_up(block, carry):
        rows = pl.ds(pl.multiple_of(block * 128, 128), 128)
        up_t[:, rows] = up_w[rows, :].T
        return carry

    def turn_down(owner):
        for part in range(down_rows // 128):
            rows = pl.ds(pl.multiple_of(owner * down_rows + part * 128, 128), 128)
            down_t[:, rows] = down_w[rows, :].T

    def turn_arrived(step):
        for way, hops in ways:
            if step > 0 and step <= hops:
                turn_down(owner_at(way, step))

    def rest_arrived(step):
        for way, hops in ways:
            if step > 0 and step <= hops:
                gather_copy(1, 1, way, step - 1, True).wait_recv()
        turn_arrived(step)

    turn_down(z)
    blocks = width // 128
    tiles = ff // F_TILE
    for step in range(1, hops_a + LAG + 1):
        if step <= hops_a:
            gather_step(0, step)
        if step == hops_a:
            rest_arrivals(0, range(1, hops_a + 1))
        if step >= LAG:
            gather_step(1, step - LAG)
            done = step - LAG

            @pl.when(jnp.logical_not(early))
            def _():
                turn_arrived(done)

            @pl.when(early)
            def _():
                rest_arrived(done - DEFER)

        if step >= hops_a and step < hops_a + LAG:
            part = step - hops_a
            lax.fori_loop(
                part * tiles // LAG,
                (part + 1) * tiles // LAG,
                lambda tile, c: (hidden_tile(tile), c)[1],
                0,
            )
            lax.fori_loop(part * blocks // LAG, (part + 1) * blocks // LAG, turn_up, 0)

    @pl.when(early)
    def _():
        for step in range(hops_a - DEFER + 1, hops_a + 1):
            rest_arrived(step)

    @pl.when(s == last)
    def _():
        for c in range(CHUNKS):
            g_in[0, c] = start[:, c * chunk : (c + 1) * chunk]

    def branch_tile(tile, carry):
        cols = pl.ds(pl.multiple_of(tile * F_TILE, F_TILE), F_TILE)
        branch[:, cols] = jnp.dot(act[...], down_w[:, cols], preferred_element_type=F32)
        return carry

    @pl.when(s < 2)
    def _():
        lax.fori_loop(0, width // F_TILE, branch_tile, 0)

    landing = jnp.where(s == 0, 1, 0)

    def chain_copy(p, c):
        rows = pl.ds(pl.multiple_of(p * piece_rows, piece_rows), piece_rows)
        return pltpu.make_async_remote_copy(
            src_ref=back.at[c, rows],
            dst_ref=g_in.at[landing, c, rows],
            send_sem=chain_sems.at[0, p, c],
            recv_sem=chain_sems.at[1, p, c],
            device_id={"pipe": below},
            device_id_type=MESH,
        )

    def chain_arrival(p, c, slot):
        rows = pl.ds(pl.multiple_of(p * piece_rows, piece_rows), piece_rows)
        return pltpu.make_async_remote_copy(
            src_ref=back.at[c, rows],
            dst_ref=g_in.at[slot, c, rows],
            send_sem=chain_sems.at[0, p, c],
            recv_sem=chain_sems.at[1, p, c],
            device_id={"pipe": below},
            device_id_type=MESH,
        )

    def piece(p, carry):
        rows = pl.ds(pl.multiple_of(p * piece_rows, piece_rows), piece_rows)

        total = jnp.zeros((piece_rows, 1), F32)
        for c in range(CHUNKS):

            @pl.when(s < last)
            def _():
                chain_arrival(p, c, 0).wait_recv()

            part = slice(c * chunk, (c + 1) * chunk)
            grad = (g_in[0, c, rows].astype(F32) * scale_ref[:, part]).astype(BF16)
            bg[rows, part] = grad
            for f in range(ff // F_TILE):
                cols = slice(f * F_TILE, (f + 1) * F_TILE)
                act_grad = jnp.dot(grad, down_t[part, cols], preferred_element_type=F32)
                if c > 0:
                    act_grad = act_grad + partial[:, cols]
                if c < CHUNKS - 1:
                    partial[:, cols] = act_grad
                else:
                    rounded = (act_grad * slope[rows, cols]).astype(BF16)
                    hg[rows, cols] = rounded
                    total += jnp.sum(
                        rounded.astype(F32) * hidden[rows, cols], axis=-1, keepdims=True
                    )
        mean = total * (1.0 / width)
        inv = inverse[rows, 0:1]
        hidden_grad = hg[rows, :]
        for c in range(CHUNKS):
            cols = slice(c * chunk, (c + 1) * chunk)
            normed_grad = jnp.dot(hidden_grad, up_t[:, cols], preferred_element_type=F32)
            unit_part = unit[rows, cols]
            back[c, rows] = (
                g_in[0, c, rows].astype(F32)
                + inv * (normed_grad * gain_ref[:, cols] - unit_part * mean)
            ).astype(BF16)
            chain_copy(p, c).start()
            gain_acc[:, cols] += jnp.sum(normed_grad * unit_part, axis=0, keepdims=True)
        return carry

    lax.fori_loop(0, PIECES, piece, 0)

    @pl.when(s >= 2)
    def _():
        lax.fori_loop(0, width // F_TILE, branch_tile, 0)

    stats[z, 0:1, :] = gain_acc[...]
    for c in range(CHUNKS):
        cols = slice(c * chunk, (c + 1) * chunk)
        stats[z, 1:2, cols] = jnp.sum(
            g_in[0, c].astype(F32) * branch[:, cols], axis=0, keepdims=True
        )

    rest = down_rows // 4
    main = down_rows - rest
    half = width // 2
    slots = (
        (rs_send_a, rs_recv_a, rest_in_a, rest_send_a, rest_recv_a, rest_own_a),
        (rs_send_b, rs_recv_b, rest_in_b, rest_send_b, rest_recv_b, rest_own_b),
    )

    def own_part(dest, first, size, cols):
        rows = pl.ds(pl.multiple_of(dest * down_rows + first, 32), size)
        return jnp.dot(act_t[rows, :], bg[:, cols], preferred_element_type=F32)

    def rs_copy(way, side, size, j):
        sent, received = slots[way][:2]
        return pltpu.make_async_remote_copy(
            src_ref=sent.at[side, j, pl.ds(0, size)],
            dst_ref=received.at[side, j, pl.ds(0, size)],
            send_sem=rs_sems.at[0, side, way, j],
            recv_sem=rs_sems.at[1, side, way, j],
            device_id=target_of(way),
            device_id_type=MESH,
        )

    def rest_copy(way, j):
        return pltpu.make_async_remote_copy(
            src_ref=slots[way][5].at[j],
            dst_ref=slots[way][2].at[j],
            send_sem=rest_sems.at[0, way, j],
            recv_sem=rest_sems.at[1, way, j],
            device_id={"pipe": other},
            device_id_type=MESH,
        )

    def rest_ring_copy(way, j):
        return pltpu.make_async_remote_copy(
            src_ref=slots[way][2].at[0] if j == 0 else slots[way][3].at[j],
            dst_ref=slots[way][4].at[j],
            send_sem=rest_ring_sems.at[0, way, j],
            recv_sem=rest_ring_sems.at[1, way, j],
            device_id=target_of(way),
            device_id_type=MESH,
        )

    def back_copy():
        return pltpu.make_async_remote_copy(
            src_ref=rest_out,
            dst_ref=rest_back,
            send_sem=back_sems.at[0],
            recv_sem=back_sems.at[1],
            device_id={"pipe": partner},
            device_id_type=MESH,
        )

    def stat_copy(way, j, arrival=False):
        ahead = j + 1 if arrival else j
        owner = lax.rem(z - ahead + ring, ring) if way == 0 else lax.rem(z + ahead, ring)
        return pltpu.make_async_remote_copy(
            src_ref=stats.at[owner],
            dst_ref=stats.at[owner],
            send_sem=stat_sems.at[0, way, j],
            recv_sem=stat_sems.at[1, way, j],
            device_id={"dp": right if way == 0 else left},
            device_id_type=MESH,
        )

    sides = (slice(0, half), slice(half, width))

    def rs_part(way, side, size, j, dest):
        sent, received = slots[way][:2]
        value = own_part(dest, 0, size, sides[side])

        @pl.when(j == 0)
        def _():
            sent[side, j, 0:size] = value.astype(BF16)

        @pl.when(j > 0)
        def _():
            rs_copy(way, side, size, j - 1).wait_recv()
            sent[side, j, 0:size] = (
                value + received[side, j - 1, 0:size].astype(F32)
            ).astype(BF16)

        rs_copy(way, side, size, j).start()

    def rest_part(way, j):
        hops = ways[way][1]

        @pl.when(j < hops)
        def _():
            dest = owner_at(1 - way, hops - j)
            for cols in sides:
                slots[way][5][j, :, cols] = own_part(dest, main, rest, cols).astype(BF16)
            rest_copy(way, j).start()

    def rs_step(j, size):
        for side in range(2):
            for way, hops in ways:

                @pl.when(j < hops)
                def _():
                    rs_part(way, side, size, j, owner_at(1 - way, hops - j))

        for way, hops in ways:

            @pl.when(j < hops)
            def _():
                @pl.when(j > 0)
                def _():
                    stat_copy(way, j - 1, True).wait_recv()

                stat_copy(way, j).start()

    def rs_step_late(j, carry):
        @pl.when(j < hops_a // 2)
        def _():
            for ahead in range(2):
                for way in range(2):
                    rest_part(way, 2 * j + ahead)

        rs_step(j, main)
        return carry

    def rs_step_full(j, carry):
        rs_step(j, down_rows)
        return carry

    def finish(size):
        for side in range(2):
            cols = sides[side]
            value = own_sum[0:size, cols]
            for way, hops in ways:
                rs_copy(way, side, size, hops - 1).wait_recv()
                value = value + slots[way][1][side, hops - 1, 0:size].astype(F32)
            out_ref[0, 0:size, cols] = value.astype(BF16)

    @pl.when(late)
    def _():
        lax.fori_loop(0, hops_a, rs_step_late, 0)
        for cols in sides:
            own_sum[:, cols] = own_part(z, 0, down_rows, cols)
        finish(main)
        back_copy().wait_recv()
        out_ref[0, main:] = (own_sum[main:] + rest_back[...].astype(F32)).astype(BF16)

    @pl.when(jnp.logical_not(late))
    def _():
        lax.fori_loop(0, hops_a, rs_step_full, 0)
        for cols in sides:
            own_sum[:, cols] = own_part(z, 0, down_rows, cols)
        finish(down_rows)


    @pl.when(early)
    def _():
        for j in range(hops_a):
            for way, hops in ways:
                if j < hops:
                    rest_copy(way, j).wait_recv()
                    if j > 0:
                        rest_ring_copy(way, j - 1).wait_recv()
                        slots[way][3][j] = (
                            slots[way][2][j].astype(F32) + slots[way][4][j - 1].astype(F32)
                        ).astype(BF16)
                    rest_ring_copy(way, j).start()
        total = jnp.zeros((rest, width), F32)
        for way, hops in ways:
            rest_ring_copy(way, hops - 1).wait_recv()
            total = total + slots[way][4][hops - 1].astype(F32)
        rest_out[...] = total.astype(BF16)
        back_copy().start()

    for way, hops in ways:
        stat_copy(way, hops - 1, True).wait_recv()
    summed = stats[0]
    for i in range(1, ring):
        summed = summed + stats[i]
    gain_out[...] = summed[0:1]
    scale_out[...] = summed[1:2]

    for way, hops in ways:
        for step in range(hops):
            for kind in range(2):
                gather_copy(kind, 0, way, step).wait_send()
            stat_copy(way, step).wait_send()

    @pl.when(jnp.logical_not(early))
    def _():
        for way, hops in ways:
            for step in range(hops):
                for kind in range(2):
                    gather_copy(kind, 1, way, step).wait_send()

    @pl.when(jnp.logical_not(late))
    def _():
        for way, hops in ways:
            for step in range(hops):
                for side in range(2):
                    rs_copy(way, side, down_rows, step).wait_send()

    @pl.when(early)
    def _():
        for kind in range(2):
            seed_copy(kind).wait_send()
        for way, hops in ways:
            for step in range(hops):
                rest_ring_copy(way, step).wait_send()
        back_copy().wait_send()

    @pl.when(late)
    def _():
        for way, hops in ways:
            for step in range(hops):
                for kind in range(2):
                    help_copy(kind, way, step).wait_send()
                    forward_copy(kind, way, step).wait_send()
                for side in range(2):
                    rs_copy(way, side, main, step).wait_send()
                rest_copy(way, step).wait_send()

    for p in range(PIECES):
        for c in range(CHUNKS):
            chain_copy(p, c).wait_send()

    @pl.when(s == last)
    def _():
        for p in range(PIECES):
            for c in range(CHUNKS):
                chain_arrival(p, c, 1).wait_recv()


def shards(stages, ring, x_saved, up_weights, down_weights, norm_gain, layer_scale, cotangent, lengths):
    unused, rows, width = x_saved.shape
    ff = up_weights.shape[2]
    down_rows = down_weights.shape[1]
    tokens = rows * 5 // 8
    hops_a = ring // 2
    hops_b = ring - 1 - hops_a
    vmem = pl.BlockSpec(memory_space=pltpu.VMEM)
    smem = pl.BlockSpec(memory_space=pltpu.SMEM)
    return pl.pallas_call(
        functools.partial(kernel, stages, ring),
        out_shape=(
            jax.ShapeDtypeStruct((1, down_rows, width), BF16),
            jax.ShapeDtypeStruct((1, width), F32),
            jax.ShapeDtypeStruct((1, width), F32),
        ),
        in_specs=[smem] + [vmem] * 6,
        out_specs=(vmem, vmem, vmem),
        scratch_shapes=[
            pltpu.VMEM((width, ff), BF16),
            pltpu.VMEM((ff, width), BF16),
            pltpu.VMEM((ff, width), BF16),
            pltpu.VMEM((width, ff), BF16),
            pltpu.VMEM((tokens, ff), F32),
            pltpu.VMEM((tokens, ff), F32),
            pltpu.VMEM((tokens, ff), BF16),
            pltpu.VMEM((ff, tokens), BF16),
            pltpu.VMEM((tokens, width), F32),
            pltpu.VMEM((tokens, 128), F32),
            pltpu.VMEM((tokens, width), BF16),
            pltpu.VMEM((tokens, width), F32),
            pltpu.VMEM((tokens, width), BF16),
            pltpu.VMEM((2, CHUNKS, tokens, width // CHUNKS), BF16),
            pltpu.VMEM((CHUNKS, tokens, width // CHUNKS), BF16),
            pltpu.VMEM((tokens, width), BF16),
            pltpu.VMEM((tokens, ff), BF16),
            pltpu.VMEM((1, width), F32),
            pltpu.VMEM((tokens // PIECES, ff), F32),
            pltpu.VMEM((ring, 2, width), F32),
            pltpu.VMEM((2, hops_a, down_rows, width // 2), BF16),
            pltpu.VMEM((2, hops_a, down_rows, width // 2), BF16),
            pltpu.VMEM((2, hops_b, down_rows, width // 2), BF16),
            pltpu.VMEM((2, hops_b, down_rows, width // 2), BF16),
            pltpu.VMEM((hops_a, down_rows // 4, width), BF16),
            pltpu.VMEM((hops_b, down_rows // 4, width), BF16),
            pltpu.VMEM((down_rows, width), F32),
            pltpu.VMEM((width // 4, ff), BF16),
            pltpu.VMEM((ff * 3 // 8, width), BF16),
            pltpu.VMEM((hops_a, down_rows // 4, width), BF16),
            pltpu.VMEM((hops_b, down_rows // 4, width), BF16),
            pltpu.VMEM((hops_a, down_rows // 4, width), BF16),
            pltpu.VMEM((hops_b, down_rows // 4, width), BF16),
            pltpu.VMEM((hops_a, down_rows // 4, width), BF16),
            pltpu.VMEM((hops_b, down_rows // 4, width), BF16),
            pltpu.VMEM((down_rows // 4, width), BF16),
            pltpu.VMEM((down_rows // 4, width), BF16),
            pltpu.SemaphoreType.DMA((2, 2, 2, 2, hops_a)),
            pltpu.SemaphoreType.DMA((3, 2, 2, hops_a)),
            pltpu.SemaphoreType.DMA((2, 2)),
            pltpu.SemaphoreType.DMA((2, PIECES, CHUNKS)),
            pltpu.SemaphoreType.DMA((2, 2, 2, hops_a)),
            pltpu.SemaphoreType.DMA((2, 2, hops_a)),
            pltpu.SemaphoreType.DMA((2, 2, hops_a)),
            pltpu.SemaphoreType.DMA((2,)),
            pltpu.SemaphoreType.DMA((2, 2, hops_a)),
        ],
        compiler_params=pltpu.CompilerParams(
            collective_id=0,
            has_side_effects=True,
            vmem_limit_bytes=60 * 1024 * 1024,
        ),
        name="layer_chain",
    )(lengths, up_weights, down_weights, x_saved, cotangent, norm_gain, layer_scale)


def solution(mesh):
    return jax.shard_map(
        functools.partial(shards, mesh.shape["pipe"], mesh.shape["dp"]),
        mesh=mesh,
        in_specs=(
            P("pipe", "dp", None),
            P("pipe", "dp", None),
            P("pipe", "dp", None),
            P("pipe", None),
            P("pipe", None),
            P("dp", None),
            P("dp", None),
        ),
        out_specs=(P("pipe", "dp", None), P("pipe", None), P("pipe", None)),
        check_vma=False,
    )
```
